256 devices in a mesh: sub: 32 (over z, y), ifc: 8 (over x, core).
Axes of the slice: x: 4, y: 4, z: 8, core: 2. Of those that a mesh axis runs over, the one named last changes fastest.
Arguments:
- gap: float32 [32, 1024, 128], P('sub', 'ifc'), may hold values from -6 to 6
- flexibility: float32 [32, 2, 1024, 2048], P('sub', None, 'ifc'), may hold values from -1 to 4, as said below
- stiffness: float32 [32, 2, 1024, 2048], P('sub', None, 'ifc'), may hold values from -1 to 4, as said below
- modes: float32 [32, 6, 2, 1024], P('sub', None, None, 'ifc'), may hold values from -1 to 1
- mode_counts: int32 [32], P('sub'), may hold values from 3 to 6
Outputs:
- multipliers: float32 [32, 1024, 128], P('sub', 'ifc')
- residual: float32 [32, 1024, 128], P('sub', 'ifc')
The draws below stay inside these ranges and needn't reach their ends.
Inputs may be any that keep to these rules, and one draw needn't show every extreme that they name: `flexibility`: each subdomain's block, as a matrix of order 2 * 1024, is symmetric positive definite. `stiffness`: each subdomain's block, as a matrix of order 2 * 1024, is symmetric positive definite.
All inputs are finite; a program needn't handle non-finite values.
Results may differ from the reference program's by a relative error of at most 0.0003.
Values sent between devices are 32-bit elements; how exact they have to be, the bound alone decides.
No kernel may reach another device: no remote copies, remote signals or barrier semaphores. Data moves between devices by JAX's collectives and lax.ppermute only.
A program may use at most 64 MiB of HBM per device.

```python
import math
import jax
import jax.numpy as jnp
from jax import lax

FACE = 1024
MODES = 6
LOADS = 128
ITERS = 1
SUBS = 32


def spd_block(key):
    order = 2 * FACE
    key_off, key_diag = jax.random.split(key)
    bound_off = 0.5 / math.sqrt(order)
    offdiag = jax.random.uniform(key_off, (SUBS, order, order), jnp.float32, -bound_off, bound_off)
    diagonal = jax.random.uniform(key_diag, (SUBS, order), jnp.float32, 1.0, 2.0)
    symmetric = (offdiag + jnp.swapaxes(offdiag, 1, 2)) * 0.5
    matrix = symmetric + jnp.eye(order, dtype=jnp.float32)[None] * diagonal[:, :, None]
    return matrix.reshape(SUBS, 2, FACE, 2 * FACE)


def draw_flexibility(key, part):
    return spd_block(jax.random.fold_in(key, 101))


def draw_stiffness(key, part):
    return spd_block(jax.random.fold_in(key, 202))


def draw_modes(key, part):
    key_base, key_right, key_left = jax.random.split(jax.random.fold_in(key, 303), 3)
    shape = (SUBS, MODES, FACE)
    base = jnp.clip(jax.random.normal(key_base, shape, jnp.float32), -5.0, 5.0)
    right_noise = jnp.clip(jax.random.normal(key_right, shape, jnp.float32), -5.0, 5.0)
    left_noise = jnp.clip(jax.random.normal(key_left, shape, jnp.float32), -5.0, 5.0)
    right_face = base + 0.1 * right_noise
    left_face = jnp.roll(base, 1, axis=0) + 0.1 * left_noise
    scale = 1.0 / math.sqrt(2.0 * FACE)
    return jnp.stack([left_face, right_face], 2) * scale


def set_ends(entries, key, least, largest):
    dims = entries.shape
    index_at = [jax.random.randint(jax.random.fold_in(key, axis), (), 0, dims[axis]) for axis in range(len(dims))]
    entries = entries.at[tuple(index_at)].set(least)
    longest = dims.index(max(dims))
    index_at[longest] = (index_at[longest] + 1) % dims[longest]
    return entries.at[tuple(index_at)].set(largest)


def block_levels(own_key, extent, cuts, low, high):
    gain, own = 1.0, jax.random.fold_in(own_key, 6)
    for axis_at, parts in cuts:
        heights = jnp.exp(jax.random.uniform(jax.random.fold_in(own, axis_at), (parts,), jnp.float32, low / len(cuts), high / len(cuts)))
        gain = gain * jnp.repeat(heights, extent[axis_at] // parts).reshape([-1 if axis == axis_at else 1 for axis in range(len(extent))])
    return gain


def bell_draw(rng, shape, width, reach, pieces=(), kind=jnp.bfloat16):
    entries = width * jax.random.normal(rng, shape, jnp.float32)
    if pieces:
        entries = entries * block_levels(rng, shape, pieces, -0.22, 0.18)
    return jnp.clip(entries, -reach, reach).astype(kind)


def setup_inputs(seed: int = 0) -> dict:
    key_of = jax.random.split(jax.random.key(seed), 6)
    return {
        "gap": bell_draw(key_of[0], (SUBS, FACE, LOADS), 1.0, 6.0, ((0, 32), (1, 8)), jnp.float32),
        "flexibility": draw_flexibility(jax.random.fold_in(key_of[5], 71), 0),
        "stiffness": draw_stiffness(jax.random.fold_in(key_of[5], 71), 0),
        "modes": draw_modes(jax.random.fold_in(key_of[5], 71), 0),
        "mode_counts": set_ends(jax.random.randint(key_of[4], (SUBS,), 3, 7), jax.random.fold_in(key_of[4], 1), 3, 6).astype(jnp.int32),
    }


precise = lax.Precision.HIGHEST

def assemble(own_blocks, next_blocks, off_blocks):
    subs_count = own_blocks.shape[0]
    mode_count = own_blocks.shape[1]
    shifted = jnp.concatenate([jnp.zeros((1, mode_count, mode_count), jnp.float32), next_blocks[:-1]], 0)
    diag_blocks = own_blocks + shifted
    ident = jnp.eye(subs_count, dtype=jnp.float32)
    upper = jnp.eye(subs_count, k=1, dtype=jnp.float32)
    whole = jnp.einsum('st,sij->sitj', ident, diag_blocks, precision=precise)
    whole = whole + jnp.einsum('st,sij->sitj', upper, off_blocks, precision=precise)
    whole = whole + jnp.einsum('st,sij->tjsi', upper, off_blocks, precision=precise)
    return whole.reshape(subs_count * mode_count, subs_count * mode_count)

def coarse_solve(factor, rhs_matrix):
    forward = lax.linalg.triangular_solve(factor, rhs_matrix, left_side=True, lower=True)
    return lax.linalg.triangular_solve(factor, forward, left_side=True, lower=True, transpose_a=True)

def reference(gap, flexibility, stiffness, modes, mode_counts):
    edge_live = (jnp.arange(SUBS) < SUBS - 1).astype(jnp.float32)[:, None, None]
    active = (jnp.arange(MODES)[None, :] < mode_counts[:, None]).astype(jnp.float32)
    mode_right = modes[:, :, 1] * active[:, :, None] * edge_live
    mode_left = modes[:, :, 0] * active[:, :, None]
    mode_next = jnp.concatenate([mode_left[1:], jnp.zeros((1, MODES, FACE), jnp.float32)], 0)
    own_blocks = jnp.einsum('smi,sni->smn', mode_right, mode_right, precision=precise)
    own_blocks = own_blocks + jnp.eye(MODES, dtype=jnp.float32)[None] * (1.0 - active)[:, :, None]
    next_blocks = jnp.einsum('smi,sni->smn', mode_next, mode_next, precision=precise)
    off_blocks = -jnp.einsum('smi,sni->smn', mode_right, mode_next, precision=precise)
    factor = jnp.linalg.cholesky(assemble(own_blocks, next_blocks, off_blocks))

    def project(vector):
        own_part = jnp.einsum('smi,sik->smk', mode_right, vector, precision=precise)
        next_part = -jnp.einsum('smi,sik->smk', mode_next, vector, precision=precise)
        coarse_rhs = own_part + jnp.concatenate([jnp.zeros((1, MODES, LOADS), jnp.float32), next_part[:-1]], 0)
        weights = coarse_solve(factor, coarse_rhs.reshape(SUBS * MODES, LOADS)).reshape(SUBS, MODES, LOADS)
        later = jnp.concatenate([weights[1:], jnp.zeros((1, MODES, LOADS), jnp.float32)], 0)
        correction = jnp.einsum('smi,smk->sik', mode_right, weights, precision=precise)
        correction = correction - jnp.einsum('smi,smk->sik', mode_next, later, precision=precise)
        return vector - correction

    def apply_jump(matrix, vector):
        before = jnp.concatenate([jnp.zeros((1, FACE, LOADS), jnp.float32), vector[:-1]], 0)
        traces = jnp.stack([-before, vector], 1).reshape(SUBS, 2 * FACE, LOADS)
        image = jnp.einsum('sim,smk->sik', matrix.reshape(SUBS, 2 * FACE, 2 * FACE), traces, precision=precise)
        image = image.reshape(SUBS, 2, FACE, LOADS)
        after = jnp.concatenate([image[1:, 0], jnp.zeros((1, FACE, LOADS), jnp.float32)], 0)
        return (image[:, 1] - after) * edge_live

    def inner(first_vec, second_vec):
        return jnp.sum(first_vec * second_vec, axis=(0, 1))

    def precond(vector):
        return project(0.25 * apply_jump(stiffness, vector))
    multipliers = jnp.zeros((SUBS, FACE, LOADS), jnp.float32)
    residual = project(gap * edge_live)
    search = precond(residual)
    direction = search
    rz_now = inner(residual, search)
    for iteration in range(ITERS):
        image = project(apply_jump(flexibility, direction))
        step_size = rz_now / inner(direction, image)
        multipliers = multipliers + step_size * direction
        residual = residual - step_size * image
        if iteration + 1 < ITERS:
            search = precond(residual)
            rz_new = inner(residual, search)
            direction = search + rz_new / rz_now * direction
            rz_now = rz_new
    return (multipliers, residual)
```

```python
import jax
import jax.numpy as jnp
from jax import lax
from jax.experimental import pallas as pl
from jax.experimental.pallas import tpu as pltpu
from jax.sharding import Mesh
from jax.sharding import PartitionSpec as P

SUB = ("z", "y")
IFC = ("x", "c")
HIGH = lax.Precision.HIGHEST
PAD = 8


def dot(a, b):
    return jnp.dot(a, b, precision=HIGH, preferred_element_type=jnp.float32)


def dot_nt(a, b):
    return lax.dot_general(
        a, b, (((1,), (1,)), ((), ())), precision=HIGH, preferred_element_type=jnp.float32
    )


def inverse_kernel(subs, modes, m_ref, out_ref, cols_ref):
    lanes = 128
    for i in range(PAD):
        rows = m_ref[pl.ds(i, subs, stride=PAD), :]
        turned = jnp.concatenate([rows] * (lanes // subs), axis=0).T
        cols_ref[pl.ds(i, 3 * PAD, stride=PAD), :] = turned[: 3 * PAD]

    def column(b, j):
        start = (b * PAD + j) * PAD
        return cols_ref[start : start + PAD, :]

    sublane = lax.broadcasted_iota(jnp.int32, (PAD, lanes), 0)
    lane = lax.broadcasted_iota(jnp.int32, (PAD, lanes), 1)
    lane_mode = lane // subs
    row_sub = lax.broadcasted_iota(jnp.int32, (subs, lanes), 0)
    lane_sub = lax.broadcasted_iota(jnp.int32, (subs, lanes), 1) % subs

    def inverse(a):
        a = list(a)
        for k in range(modes):
            pivot = 1.0 / a[k][k : k + 1, :]
            is_k = sublane == k
            for j in range(modes):
                if j != k:
                    scaled = a[j][k : k + 1, :] * pivot
                    a[j] = jnp.where(is_k, scaled, a[j] - a[k] * scaled)
            a[k] = jnp.where(is_k, pivot, -a[k] * pivot)
        return a

    def product(a, b):
        out = []
        for j in range(modes):
            total = a[0] * b[j][0:1, :]
            for k in range(1, modes):
                total = total + a[k] * b[j][k : k + 1, :]
            out.append(total)
        return out

    def moved(a, shift):
        return [pltpu.roll(x, shift % lanes, 1) for x in a]

    def dense(parts):
        halves = []
        for half in range(2):
            rows_of = []
            for a, shift in parts:
                chosen = jnp.zeros((PAD, lanes), jnp.float32)
                for q in range(lanes // subs):
                    k = half * (lanes // subs) + q
                    if k < modes:
                        chosen = jnp.where(lane_mode == q, a[k], chosen)
                rows_of.append((chosen, row_sub == lane_sub + shift))
            strips = []
            for i in range(PAD):
                strip = jnp.zeros((subs, lanes), jnp.float32)
                for chosen, mask in rows_of:
                    strip = jnp.where(mask, chosen[i : i + 1, :], strip)
                strips.append(strip)
            halves.append(jnp.concatenate(strips, axis=0))
        return jnp.concatenate(halves, axis=1)

    lower = [column(0, j) for j in range(modes)]
    diag = [column(1, j) for j in range(modes)]
    upper = [column(2, j) for j in range(modes)]
    ident = [jnp.where(sublane == k, 1.0, 0.0) for k in range(modes)]
    total = None
    h = 1
    while h < subs:
        inv = inverse(diag)
        alpha = product(lower, moved(inv, h))
        gamma = product(upper, moved(inv, -h))
        upper_before, lower_before = moved(upper, h), moved(lower, h)
        upper_after, lower_after = moved(upper, -h), moved(lower, -h)
        first = product(alpha, upper_before)
        second = product(gamma, lower_after)
        diag = [d - f - g for d, f, g in zip(diag, first, second)]
        lower = [-x for x in product(alpha, lower_before)]
        upper = [-x for x in product(gamma, upper_after)]
        step = dense(
            [
                (ident, 0),
                ([-x for x in moved(alpha, -h)], h),
                ([-x for x in moved(gamma, h)], -h),
            ]
        )
        total = step if total is None else dot(step, total)
        h *= 2
    out_ref[...] = dot(dense([(inverse(diag), 0)]), total)


def coarse_inverse(rows, subs, modes):
    size = subs * PAD
    return pl.pallas_call(
        lambda *refs: inverse_kernel(subs, modes, *refs),
        out_shape=jax.ShapeDtypeStruct((size, size), jnp.float32),
        in_specs=[pl.BlockSpec(memory_space=pltpu.VMEM)],
        out_specs=pl.BlockSpec(memory_space=pltpu.VMEM),
        scratch_shapes=[pltpu.VMEM((3 * PAD * PAD, 128), jnp.float32)],
        name="coarse_inverse",
    )(rows)


def moved_along(block, distance):
    n = lax.axis_size(SUB)
    return lax.ppermute(
        block, SUB, [(i - distance, i) for i in range(n) if 0 <= i - distance < n]
    )


def core_swap(block):
    return lax.ppermute(block, "c", [(0, 1), (1, 0)])


def from_all(value, axis):
    count = lax.axis_size(axis)
    return lax.all_to_all(
        jnp.broadcast_to(value[None], (count, *value.shape)), axis, 0, 0, tiled=True
    )


def gathered(piece):
    own = from_all(piece, "x")
    other = core_swap(own)
    on_first = lax.axis_index("c") == 0
    return jnp.stack([jnp.where(on_first, own, other), jnp.where(on_first, other, own)], 1)


def per_device(gap, flexibility, stiffness, modes, mode_counts):
    subs = lax.axis_size(SUB)
    sub = lax.axis_index(SUB)
    rows, loads = gap.shape[1], gap.shape[2]
    lanes = lax.axis_size(IFC)
    face = rows * lanes
    mode_count = modes.shape[1]
    live = (sub < subs - 1).astype(jnp.float32)
    inner = (sub > 0).astype(jnp.float32)
    flex = flexibility.reshape(2 * rows, 2 * face)
    stiff = stiffness.reshape(2 * rows, 2 * face)

    active = (jnp.arange(PAD) < jnp.minimum(mode_counts[0], mode_count)).astype(jnp.float32)
    padded = jnp.pad(modes[0], ((0, PAD - mode_count), (0, 0), (0, 0))) * active[:, None, None]
    left, right = padded[:, 0], padded[:, 1] * live
    field = gap[0] * live

    from_before = moved_along(jnp.concatenate([field, right], 0), 1)
    left_after = moved_along(left, -1)
    field_before, right_before = from_before[:rows], from_before[rows:]
    piece = jnp.concatenate(
        [-field_before, field, -right_before, left * inner, right, -left_after], 0
    )
    whole = gathered(piece)

    def traces_of(pieces):
        pieces = pieces.reshape(lanes, 2, rows, loads)
        return pieces.transpose(1, 0, 2, 3).reshape(2 * face, loads)

    gap_traces = traces_of(whole[:, :, : 2 * rows])
    faces = whole[:, :, 2 * rows :].reshape(lanes, 4, PAD, rows)
    faces = faces.transpose(1, 2, 0, 3).reshape(4, PAD, face)
    none = jnp.zeros((PAD, face), jnp.float32)
    basis = jnp.concatenate(
        [
            jnp.concatenate([faces[0], faces[1], none], 0),
            jnp.concatenate([none, faces[2], faces[3]], 0),
        ],
        1,
    )
    own_basis = jnp.concatenate(
        [
            jnp.concatenate([-right_before, left * inner, jnp.zeros_like(left)], 0),
            jnp.concatenate([jnp.zeros_like(left), right, -left_after], 0),
        ],
        1,
    )
    here = basis[PAD : 2 * PAD]

    rest = jnp.pad(
        jnp.eye(PAD, dtype=jnp.float32) * (1.0 - active)[:, None], ((0, 0), (PAD, PAD))
    )
    blocks = dot_nt(here, basis) + rest
    rhs = dot(here, gap_traces)
    sent = jnp.concatenate([rhs, jnp.pad(blocks, ((0, 0), (0, 128 - 3 * PAD)))], 0)
    first = from_all(sent, SUB)
    inverse = coarse_inverse(first[:, PAD:].reshape(subs * PAD, 128), subs, mode_count)
    near = jnp.pad(inverse.reshape(PAD, subs, PAD * subs), ((0, 0), (1, 1), (0, 0)))
    near = lax.dynamic_slice_in_dim(near, sub, 3, 1)
    near = near.transpose(1, 0, 2).reshape(3 * PAD, PAD * subs)

    def weights_of(all_rhs):
        return dot(near, all_rhs.transpose(1, 0, 2).reshape(PAD * subs, loads))

    def spread(part, weights):
        return lax.dot_general(
            part, weights, (((0,), (0,)), ((), ())), precision=HIGH,
            preferred_element_type=jnp.float32,
        )

    weights = weights_of(first[:, :PAD])
    res_traces = gap_traces - spread(basis, weights)
    own_res = field - spread(own_basis[:, rows:], weights)

    image = 0.25 * dot(stiff, res_traces)
    before = moved_along(image[rows:], 1)
    after = moved_along(image[:rows], -1)
    own_search = (image[rows:] - after) * live
    before_search = (before - image[:rows]) * inner
    own_traces = jnp.concatenate([-before_search, own_search], 0)
    search_traces = traces_of(gathered(own_traces))
    second = from_all(dot(here, search_traces), SUB)
    pre_image = dot(flex, search_traces)
    flex_basis = dot_nt(flex, basis)
    weights = weights_of(second)
    image = pre_image - dot(flex_basis, weights)
    direction = own_traces - spread(own_basis, weights)

    after = moved_along(image[:rows], -1)
    sums = jnp.stack(
        [jnp.sum(own_res * own_search, 0), jnp.sum(direction * image, 0)], 0
    )
    partial = jnp.concatenate([dot(own_basis, image), jnp.pad(sums, ((0, PAD - 2), (0, 0)))], 0)
    partial = partial + core_swap(partial)
    partial = from_all(partial, "x").sum(0)
    third = from_all(partial, SUB)
    totals = third[:, 3 * PAD :].sum(0)
    parts = third[:, : 3 * PAD].reshape(subs, 3, PAD, loads)
    none = jnp.zeros((1, PAD, loads), jnp.float32)
    all_rhs = (
        parts[:, 1]
        + jnp.concatenate([parts[1:, 0], none], 0)
        + jnp.concatenate([none, parts[:-1, 2]], 0)
    )
    weights = weights_of(all_rhs)
    step = totals[0] / totals[1]
    own_image = (image[rows:] - after) * live - spread(own_basis[:, rows:], weights)
    return (step * direction[rows:])[None], (own_res - step * own_image)[None]


def solution(mesh):
    finer = Mesh(mesh.devices.reshape(8, 4, 4, 2), ("z", "y", "x", "c"))
    return jax.shard_map(
        per_device,
        mesh=finer,
        in_specs=(
            P(SUB, IFC, None),
            P(SUB, None, IFC, None),
            P(SUB, None, IFC, None),
            P(SUB, None, None, IFC),
            P(SUB),
        ),
        out_specs=(P(SUB, IFC, None), P(SUB, IFC, None)),
        check_vma=False,
    )
```

```python
import jax
import jax.numpy as jnp
from jax import lax
from jax.experimental import pallas as pl
from jax.experimental.pallas import tpu as pltpu
from jax.sharding import Mesh
from jax.sharding import PartitionSpec as P


SUB = ("z", "y")
IFC = ("x", "c")
ALL = SUB + IFC
HIGH = lax.Precision.HIGHEST
NEAR = 5
PAD = 8


def dot(a, b):
    return jnp.dot(a, b, precision=HIGH, preferred_element_type=jnp.float32)


def dot_nt(a, b):
    return lax.dot_general(
        a, b, (((1,), (1,)), ((), ())), precision=HIGH, preferred_element_type=jnp.float32
    )


def inverse_kernel(subs, modes, sub_ref, sent_ref, inverse_ref, near_ref, weights_ref, cols_ref):
    lanes = 128
    for i in range(PAD):
        rows = sent_ref[pl.ds(PAD + i, subs, stride=2 * PAD), :]
        turned = jnp.concatenate([rows] * (lanes // subs), axis=0).T
        cols_ref[pl.ds(i, 3 * PAD, stride=PAD), :] = turned[: 3 * PAD]

    def column(b, j):
        start = (b * PAD + j) * PAD
        return cols_ref[start : start + PAD, :]

    sublane = lax.broadcasted_iota(jnp.int32, (PAD, lanes), 0)
    lane = lax.broadcasted_iota(jnp.int32, (PAD, lanes), 1)
    lane_mode = lane // subs
    row_sub = lax.broadcasted_iota(jnp.int32, (subs, lanes), 0)
    lane_sub = lax.broadcasted_iota(jnp.int32, (subs, lanes), 1) % subs

    def inverse(a):
        a = list(a)
        for k in range(modes):
            pivot = 1.0 / a[k][k : k + 1, :]
            is_k = sublane == k
            for j in range(modes):
                if j != k:
                    scaled = a[j][k : k + 1, :] * pivot
                    a[j] = jnp.where(is_k, scaled, a[j] - a[k] * scaled)
            a[k] = jnp.where(is_k, pivot, -a[k] * pivot)
        return a

    def product(a, b):
        out = []
        for j in range(modes):
            total = a[0] * b[j][0:1, :]
            for k in range(1, modes):
                total = total + a[k] * b[j][k : k + 1, :]
            out.append(total)
        return out

    def moved(a, shift):
        return [pltpu.roll(x, shift % lanes, 1) for x in a]

    def dense(parts):
        halves = []
        for half in range(2):
            rows_of = []
            for a, shift in parts:
                chosen = jnp.zeros((PAD, lanes), jnp.float32)
                for q in range(lanes // subs):
                    k = half * (lanes // subs) + q
                    if k < modes:
                        chosen = jnp.where(lane_mode == q, a[k], chosen)
                rows_of.append((chosen, row_sub == lane_sub + shift))
            strips = []
            for i in range(PAD):
                strip = jnp.zeros((subs, lanes), jnp.float32)
                for chosen, mask in rows_of:
                    strip = jnp.where(mask, chosen[i : i + 1, :], strip)
                strips.append(strip)
            halves.append(jnp.concatenate(strips, axis=0))
        return jnp.concatenate(halves, axis=1)

    lower = [column(0, j) for j in range(modes)]
    diag = [column(1, j) for j in range(modes)]
    upper = [column(2, j) for j in range(modes)]
    ident = [jnp.where(sublane == k, 1.0, 0.0) for k in range(modes)]
    total = None
    h = 1
    while h < subs:
        inv = inverse(diag)
        alpha = product(lower, moved(inv, h))
        gamma = product(upper, moved(inv, -h))
        upper_before, lower_before = moved(upper, h), moved(lower, h)
        upper_after, lower_after = moved(upper, -h), moved(lower, -h)
        first = product(alpha, upper_before)
        second = product(gamma, lower_after)
        diag = [d - f - g for d, f, g in zip(diag, first, second)]
        lower = [-x for x in product(alpha, lower_before)]
        upper = [-x for x in product(gamma, upper_after)]
        step = dense(
            [
                (ident, 0),
                ([-x for x in moved(alpha, -h)], h),
                ([-x for x in moved(gamma, h)], -h),
            ]
        )
        total = step if total is None else dot(step, total)
        h *= 2
    whole = dot(dense([(inverse(diag), 0)]), total)
    inverse_ref[...] = whole
    row = lax.broadcasted_iota(jnp.int32, (NEAR * PAD, PAD * subs), 0)
    col = lax.broadcasted_iota(jnp.int32, (NEAR * PAD, PAD * subs), 1)
    wanted = (row % PAD) * subs + row // PAD + (sub_ref[0] - NEAR // 2)
    inside = (row // PAD + sub_ref[0] >= NEAR // 2) & (row // PAD + sub_ref[0] < subs + NEAR // 2)
    near = dot(jnp.where((col == wanted) & inside, 1.0, 0.0), whole)
    near_ref[...] = near
    rhs = jnp.concatenate(
        [sent_ref[pl.ds(i, subs, stride=2 * PAD), :] for i in range(PAD)], axis=0
    )
    weights_ref[...] = dot(near, rhs)


def coarse_inverse(sub, sent, subs, modes):
    size = subs * PAD
    vmem = pl.BlockSpec(memory_space=pltpu.VMEM)
    return pl.pallas_call(
        lambda *refs: inverse_kernel(subs, modes, *refs),
        out_shape=[
            jax.ShapeDtypeStruct((size, size), jnp.float32),
            jax.ShapeDtypeStruct((NEAR * PAD, size), jnp.float32),
            jax.ShapeDtypeStruct((NEAR * PAD, 128), jnp.float32),
        ],
        in_specs=[pl.BlockSpec(memory_space=pltpu.SMEM), vmem],
        out_specs=[vmem] * 3,
        scratch_shapes=[pltpu.VMEM((3 * PAD * PAD, 128), jnp.float32)],
        name="coarse_inverse",
    )(sub, sent)


def assemble_kernel(count, rows, own_ref, other_ref, place_ref, traces_ref, extra_ref):
    x, core = place_ref[0], place_ref[1]
    head = 0 if traces_ref is None else 2 * rows
    for q in range(count):
        d = lax.rem(x - q + count, count)
        for c in range(2):
            at = 2 * q + c

            def copy(ref):
                if traces_ref is not None:
                    for face in range(2):
                        start = (face * 2 * count + at) * rows
                        traces_ref[start : start + rows, :] = ref[d, face * rows : (face + 1) * rows, :]
                extra_ref[:, at * 128 : (at + 1) * 128] = ref[d, head:, :]

            @pl.when(core == c)
            def _():
                copy(own_ref)

            @pl.when(core != c)
            def _():
                copy(other_ref)


def assemble(own, other, place, rows, with_traces):
    count, pieces, _ = own.shape
    vmem = pl.BlockSpec(memory_space=pltpu.VMEM)
    head = 2 * rows if with_traces else 0
    extra = jax.ShapeDtypeStruct((pieces - head, 2 * count * 128), jnp.float32)
    traces = jax.ShapeDtypeStruct((2 * rows * 2 * count, 128), jnp.float32)

    def kernel(own_ref, other_ref, place_ref, *outs):
        outs = outs if with_traces else (None, *outs)
        assemble_kernel(count, rows, own_ref, other_ref, place_ref, *outs)

    return pl.pallas_call(
        kernel,
        out_shape=[traces, extra] if with_traces else [extra],
        in_specs=[vmem, vmem, pl.BlockSpec(memory_space=pltpu.SMEM)],
        out_specs=[vmem] * (2 if with_traces else 1),
        name="assemble",
    )(own, other, place)


def moved_along(block, distance):
    n = lax.axis_size(SUB)
    return lax.ppermute(
        block, SUB, [(i - distance, i) for i in range(n) if 0 <= i - distance < n]
    )


def core_swap(block):
    return lax.ppermute(block, "c", [(0, 1), (1, 0)])


def from_all(value, axis):
    count = lax.axis_size(axis)
    return lax.all_to_all(
        jnp.broadcast_to(value[None], (count, *value.shape)), axis, 0, 0, tiled=True
    )


def along_x(piece):
    n = lax.axis_size("x")
    return [piece] + [
        lax.ppermute(piece, "x", [(i, (i + d) % n) for i in range(n)]) for d in range(1, n)
    ]


def gathered(piece, place, rows, with_traces=True):
    own = jnp.stack(along_x(piece))
    return assemble(own, core_swap(own), place, rows, with_traces)


def spread(part, weights):
    return lax.dot_general(
        part, weights, (((0,), (0,)), ((), ())), precision=HIGH, preferred_element_type=jnp.float32
    )


def per_device(gap, flexibility, stiffness, modes, mode_counts):
    subs = lax.axis_size(SUB)
    sub = lax.axis_index(SUB)
    place = jnp.stack([lax.axis_index("x"), lax.axis_index("c")]).astype(jnp.int32)
    rows, loads = gap.shape[1], gap.shape[2]
    lanes = lax.axis_size(IFC)
    face = rows * lanes
    mode_count = modes.shape[1]
    live = (sub < subs - 1).astype(jnp.float32)
    inner = (sub > 0).astype(jnp.float32)
    flex = flexibility.reshape(2 * rows, 2 * face)
    stiff = stiffness.reshape(2 * rows, 2 * face)

    active = (jnp.arange(PAD) < jnp.minimum(mode_counts[0], mode_count)).astype(jnp.float32)
    padded = jnp.pad(modes[0], ((0, PAD - mode_count), (0, 0), (0, 0))) * active[:, None, None]
    left, right = padded[:, 0], padded[:, 1] * live
    field = gap[0] * live

    from_before = moved_along(jnp.concatenate([field, right], 0), 1)
    left_after = moved_along(left, -1)
    field_before, right_before = from_before[:rows], from_before[rows:]
    left_in = left * inner
    piece = jnp.concatenate([-field_before, field, -right_before, left_in, right, -left_after], 0)
    gap_traces, faces = gathered(piece, place, rows)
    none = jnp.zeros((PAD, face), jnp.float32)
    basis = jnp.concatenate(
        [
            jnp.concatenate([faces[: 2 * PAD], none], 0),
            jnp.concatenate([none, faces[2 * PAD :]], 0),
        ],
        1,
    )
    none = jnp.zeros_like(left)
    own_basis = jnp.concatenate(
        [
            jnp.concatenate([-right_before, left_in, none], 0),
            jnp.concatenate([none, right, -left_after], 0),
        ],
        1,
    )
    here = basis[PAD : 2 * PAD]
    rest = jnp.pad(
        jnp.eye(PAD, dtype=jnp.float32) * (1.0 - active)[:, None], ((0, 0), (PAD, PAD))
    )
    blocks = dot_nt(here, basis) + rest
    rhs = dot(here, gap_traces)
    sent = jnp.concatenate([rhs, jnp.pad(blocks, ((0, 0), (0, 128 - 3 * PAD)))], 0)

    image = 0.25 * dot(stiff, gap_traces)
    modes_image = 0.25 * dot_nt(basis, stiff)
    first = from_all(sent, SUB).reshape(subs * 2 * PAD, 128)
    before = moved_along(jnp.concatenate([image[rows:], modes_image[:, rows:]], 0), 1)
    after = moved_along(jnp.concatenate([image[:rows], modes_image[:, :rows]], 0), -1)
    top = (image[:rows] - before[:rows]) * inner
    bottom = (image[rows:] - after[:rows]) * live
    own_traces = jnp.concatenate([top, bottom], 0)
    gone = jnp.zeros((PAD, rows), jnp.float32)
    modes_top = jnp.concatenate([gone, modes_image[:, :rows], gone], 0)
    modes_top = modes_top - jnp.concatenate([before[rows:], gone, gone], 0)
    modes_bottom = jnp.concatenate([gone, modes_image[:, rows:], gone], 0)
    modes_bottom = modes_bottom - jnp.concatenate([gone, gone, after[rows:]], 0)
    own_modes = jnp.concatenate([modes_top * inner, modes_bottom * live], 1)

    flex_modes = dot_nt(basis, flex)
    small = dot_nt(flex_modes, jnp.concatenate([own_modes, own_basis], 0))
    cross = jnp.pad(dot_nt(own_basis[PAD : 2 * PAD], own_modes), ((0, 2 * PAD), (0, 0)))
    small = jnp.concatenate([small, cross], 1)
    small = jnp.pad(small, ((0, 0), (0, 128 - small.shape[1])))
    piece = jnp.concatenate([own_traces, dot(flex_modes, own_traces), small], 0)
    search_traces, extra = gathered(piece, place, rows)
    extra = extra.reshape(6 * PAD, lanes, 128).sum(1)
    flex_search, small = extra[: 3 * PAD], extra[3 * PAD :]
    wide = NEAR * PAD

    inverse, near, weights = coarse_inverse(sub.astype(jnp.int32)[None], first, subs, mode_count)
    near = near[PAD : 4 * PAD]
    rhs = dot(here, search_traces) - dot(small[:PAD, wide + 3 * PAD : 2 * wide + 3 * PAD], weights)
    flex_search = flex_search - dot(small[:, :wide], weights)
    mine = (place[0] * 2 + place[1]) * (loads // lanes)
    share = loads // lanes

    def folded(block):
        return jnp.concatenate([block[b * PAD : (b + 1) * PAD] for b in range(3)], 1)

    flex_search = lax.dynamic_slice_in_dim(flex_search, mine, share, 1)
    last = jnp.concatenate([folded(flex_search), folded(small[:, wide : wide + 3 * PAD])], 1)
    last = jnp.pad(last, ((0, 0), (0, 128 - last.shape[1])))
    second = from_all(jnp.concatenate([rhs, last], 0), SUB)

    (modes_traces,) = gathered(
        jnp.concatenate([own_modes[:, :rows], own_modes[:, rows:]], 0), place, rows, False
    )
    modes_traces = jnp.concatenate([modes_traces[:wide], modes_traces[wide:]], 1)
    image = dot(flex, search_traces) - dot(dot_nt(flex, modes_traces), weights)
    own_search = own_traces - spread(own_modes, weights)
    own_res = field - spread(own_basis[:, rows:], weights[PAD : 4 * PAD])

    all_rhs = second[:, :PAD].transpose(1, 0, 2).reshape(PAD * subs, loads)
    weights = dot(near, all_rhs)
    image = image - spread(flex_modes, weights)
    direction = own_search - spread(own_basis, weights)
    sums = jnp.stack(
        [jnp.sum(own_res * own_search[rows:], 0), jnp.sum(direction * image, 0)], 0
    )
    totals = from_all(sums, ALL).sum(0)

    after = moved_along(image[:rows], -1)
    my_rhs = lax.dynamic_slice_in_dim(all_rhs, mine, share, 1)
    my_weights = dot(inverse, my_rhs).reshape(PAD, subs, share).transpose(1, 0, 2)
    my_weights = jnp.pad(my_weights, ((1, 1), (0, 0), (0, 0)))
    my_weights = jnp.concatenate([my_weights[b : b + subs] for b in range(3)], 1)
    tail = second[:, PAD:]
    parts = []
    for b in range(3):
        start = 3 * share + b * 3 * PAD
        product = lax.dot_general(
            tail[:, :, start : start + 3 * PAD], my_weights, (((2,), (1,)), ((0,), (0,))),
            precision=HIGH, preferred_element_type=jnp.float32,
        )
        parts.append(tail[:, :, b * share : (b + 1) * share] - product)
    none = jnp.zeros((1, PAD, share), jnp.float32)
    last_rhs = (
        parts[1]
        + jnp.concatenate([parts[0][1:], none], 0)
        + jnp.concatenate([none, parts[2][:-1]], 0)
    )
    weights = dot(near, last_rhs.transpose(1, 0, 2).reshape(PAD * subs, share))
    weights = lax.dynamic_update_slice_in_dim(
        jnp.zeros((3 * PAD, loads), jnp.float32), weights, mine, 1
    )
    weights = weights + core_swap(weights)
    weights = sum(along_x(weights))
    own_image = (image[rows:] - after) * live - spread(own_basis[:, rows:], weights)
    step = totals[0] / totals[1]
    return (step * direction[rows:])[None], (own_res - step * own_image)[None]


def solution(mesh):
    finer = Mesh(mesh.devices.reshape(8, 4, 4, 2), ALL)
    return jax.shard_map(
        per_device,
        mesh=finer,
        in_specs=(
            P(SUB, IFC, None),
            P(SUB, None, IFC, None),
            P(SUB, None, IFC, None),
            P(SUB, None, None, IFC),
            P(SUB),
        ),
        out_specs=(P(SUB, IFC, None), P(SUB, IFC, None)),
        check_vma=False,
    )
```

```python
import jax
import jax.numpy as jnp
from jax import lax
from jax.experimental import pallas as pl
from jax.experimental.pallas import tpu as pltpu
from jax.sharding import Mesh
from jax.sharding import PartitionSpec as P


SUB = ("z", "y")
IFC = ("x", "c")
ALL = SUB + IFC
HIGH = lax.Precision.HIGHEST
NEAR = 5
PAD = 8


def dot(a, b):
    return jnp.dot(a, b, precision=HIGH, preferred_element_type=jnp.float32)


def dot_nt(a, b):
    return lax.dot_general(
        a, b, (((1,), (1,)), ((), ())), precision=HIGH, preferred_element_type=jnp.float32
    )


def inverse_kernel(subs, modes, sub_ref, sent_ref, inverse_ref, near_ref, weights_ref, cols_ref):
    lanes = 128
    for i in range(PAD):
        rows = sent_ref[pl.ds(PAD + i, subs, stride=2 * PAD), :]
        turned = jnp.concatenate([rows] * (lanes // subs), axis=0).T
        cols_ref[pl.ds(i, 3 * PAD, stride=PAD), :] = turned[: 3 * PAD]

    def column(b, j):
        start = (b * PAD + j) * PAD
        return cols_ref[start : start + PAD, :]

    sublane = lax.broadcasted_iota(jnp.int32, (PAD, lanes), 0)
    lane = lax.broadcasted_iota(jnp.int32, (PAD, lanes), 1)
    lane_mode = lane // subs
    row_sub = lax.broadcasted_iota(jnp.int32, (subs, lanes), 0)
    lane_sub = lax.broadcasted_iota(jnp.int32, (subs, lanes), 1) % subs

    def inverse(a):
        a = list(a)
        for k in range(modes):
            pivot = 1.0 / a[k][k : k + 1, :]
            is_k = sublane == k
            for j in range(modes):
                if j != k:
                    scaled = a[j][k : k + 1, :] * pivot
                    a[j] = jnp.where(is_k, scaled, a[j] - a[k] * scaled)
            a[k] = jnp.where(is_k, pivot, -a[k] * pivot)
        return a

    def product(a, b):
        out = []
        for j in range(modes):
            total = a[0] * b[j][0:1, :]
            for k in range(1, modes):
                total = total + a[k] * b[j][k : k + 1, :]
            out.append(total)
        return out

    def moved(a, shift):
        return [pltpu.roll(x, shift % lanes, 1) for x in a]

    def dense(parts):
        halves = []
        for half in range(2):
            rows_of = []
            for a, shift in parts:
                chosen = jnp.zeros((PAD, lanes), jnp.float32)
                for q in range(lanes // subs):
                    k = half * (lanes // subs) + q
                    if k < modes:
                        chosen = jnp.where(lane_mode == q, a[k], chosen)
                rows_of.append((chosen, row_sub == lane_sub + shift))
            strips = []
            for i in range(PAD):
                strip = jnp.zeros((subs, lanes), jnp.float32)
                for chosen, mask in rows_of:
                    strip = jnp.where(mask, chosen[i : i + 1, :], strip)
                strips.append(strip)
            halves.append(jnp.concatenate(strips, axis=0))
        return jnp.concatenate(halves, axis=1)

    lower = [column(0, j) for j in range(modes)]
    diag = [column(1, j) for j in range(modes)]
    upper = [column(2, j) for j in range(modes)]
    ident = [jnp.where(sublane == k, 1.0, 0.0) for k in range(modes)]
    total = None
    h = 1
    while h < subs:
        inv = inverse(diag)
        alpha = product(lower, moved(inv, h))
        gamma = product(upper, moved(inv, -h))
        upper_before, lower_before = moved(upper, h), moved(lower, h)
        upper_after, lower_after = moved(upper, -h), moved(lower, -h)
        first = product(alpha, upper_before)
        second = product(gamma, lower_after)
        diag = [d - f - g for d, f, g in zip(diag, first, second)]
        lower = [-x for x in product(alpha, lower_before)]
        upper = [-x for x in product(gamma, upper_after)]
        step = dense(
            [
                (ident, 0),
                ([-x for x in moved(alpha, -h)], h),
                ([-x for x in moved(gamma, h)], -h),
            ]
        )
        total = step if total is None else dot(step, total)
        h *= 2
    whole = dot(dense([(inverse(diag), 0)]), total)
    inverse_ref[...] = whole
    row = lax.broadcasted_iota(jnp.int32, (NEAR * PAD, PAD * subs), 0)
    col = lax.broadcasted_iota(jnp.int32, (NEAR * PAD, PAD * subs), 1)
    wanted = (row % PAD) * subs + row // PAD + (sub_ref[0] - NEAR // 2)
    inside = (row // PAD + sub_ref[0] >= NEAR // 2) & (row // PAD + sub_ref[0] < subs + NEAR // 2)
    near = dot(jnp.where((col == wanted) & inside, 1.0, 0.0), whole)
    near_ref[...] = near
    rhs = jnp.concatenate(
        [sent_ref[pl.ds(i, subs, stride=2 * PAD), :] for i in range(PAD)], axis=0
    )
    weights_ref[...] = dot(near, rhs)


def coarse_inverse(sub, sent, subs, modes):
    size = subs * PAD
    vmem = pl.BlockSpec(memory_space=pltpu.VMEM)
    return pl.pallas_call(
        lambda *refs: inverse_kernel(subs, modes, *refs),
        out_shape=[
            jax.ShapeDtypeStruct((size, size), jnp.float32),
            jax.ShapeDtypeStruct((NEAR * PAD, size), jnp.float32),
            jax.ShapeDtypeStruct((NEAR * PAD, 128), jnp.float32),
        ],
        in_specs=[pl.BlockSpec(memory_space=pltpu.SMEM), vmem],
        out_specs=[vmem] * 3,
        scratch_shapes=[pltpu.VMEM((3 * PAD * PAD, 128), jnp.float32)],
        name="coarse_inverse",
    )(sub, sent)


def each_piece(count, own_ref, other_ref, place_ref, copy):
    for q in range(count):
        d = lax.rem(place_ref[0] - q + count, count)
        for c in range(2):

            @pl.when(place_ref[1] == c)
            def _():
                copy(own_ref, d, 2 * q + c)

            @pl.when(place_ref[1] != c)
            def _():
                copy(other_ref, d, 2 * q + c)


VMEM = pl.BlockSpec(memory_space=pltpu.VMEM)
SMEM = pl.BlockSpec(memory_space=pltpu.SMEM)


def shapes(*dims):
    return [jax.ShapeDtypeStruct(d, jnp.float32) for d in dims]


def stiff_kernel(count, rows, own_ref, other_ref, place_ref, rest_ref, stiff_ref, up_ref, down_ref, basis_ref,
                 sent_ref, ext_ref):
    face = 2 * count * rows
    basis_ref[2 * PAD :, :face] = jnp.zeros((PAD, face), jnp.float32)
    basis_ref[:PAD, face:] = jnp.zeros((PAD, face), jnp.float32)

    def copy(ref, d, at):
        for side in range(2):
            start = side * face + at * rows
            ext_ref[start : start + rows, :128] = ref[d, side * rows : (side + 1) * rows, :]
        lanes = slice(at * rows, (at + 1) * rows)
        basis_ref[: 2 * PAD, lanes] = ref[d, 2 * rows : 2 * rows + 2 * PAD, :]
        lanes = slice(face + at * rows, face + (at + 1) * rows)
        basis_ref[PAD:, lanes] = ref[d, 2 * rows + 2 * PAD :, :]

    each_piece(count, own_ref, other_ref, place_ref, copy)
    filler = jnp.zeros((128 - 3 * PAD, 128), jnp.float32)
    for at in range(2 * face // 128):
        lanes = slice(at * 128, (at + 1) * 128)
        ext_ref[lanes, 128:] = jnp.concatenate([basis_ref[:, lanes], filler], 0).T
    ext = ext_ref[...]
    image = 0.25 * dot(stiff_ref[...], ext)
    modes_image = image[:, 128:].T[: 3 * PAD]
    up_ref[:rows] = image[rows:, :128]
    up_ref[rows:] = modes_image[:, rows:]
    down_ref[:rows] = image[:rows, :128]
    down_ref[rows:] = modes_image[:, :rows]
    coarse = dot(basis_ref[PAD : 2 * PAD, :], ext)
    coarse = jnp.concatenate([coarse[:, :128], coarse[:, 128:] + rest_ref[...]], 0)
    for t in range(sent_ref.shape[0]):
        sent_ref[t] = coarse


def apply_stiffness(own, other, place, rest, stiff, subs):
    count, rows = own.shape[0], stiff.shape[0] // 2
    face = 2 * count * rows
    return pl.pallas_call(
        lambda *refs: stiff_kernel(count, rows, *refs),
        out_shape=shapes(
            (rows + 3 * PAD, 128), (rows + 3 * PAD, 128), (3 * PAD, 2 * face), (subs, 2 * PAD, 128)
        ),
        in_specs=[VMEM, VMEM, SMEM, VMEM, VMEM],
        out_specs=[VMEM] * 4,
        scratch_shapes=[pltpu.VMEM((2 * face, 256), jnp.float32)],
        name="apply_stiffness",
    )(own, other, place, rest, stiff)


def search_kernel(count, rows, share, own_ref, other_ref, place_ref, basis_ref, weights_ref, traces_ref,
                  modes_ref, sent_ref, sums_ref):
    face = 2 * count * rows
    wide = NEAR * PAD
    head = 2 * rows
    sums_ref[...] = own_ref[0, head : head + 7 * PAD, :] + other_ref[0, head : head + 7 * PAD, :]
    for d in range(1, count):
        sums_ref[...] += own_ref[d, head : head + 7 * PAD, :] + other_ref[d, head : head + 7 * PAD, :]

    def copy(ref, d, at):
        for side in range(2):
            start = side * face + at * rows
            traces_ref[start : start + rows, :] = ref[d, side * rows : (side + 1) * rows, :]
            low = head + 7 * PAD + side * wide
            modes_ref[:, start : start + rows] = ref[d, low : low + wide, :]

    each_piece(count, own_ref, other_ref, place_ref, copy)
    weights = jnp.concatenate([weights_ref[...], jnp.zeros((128 - wide, 128), jnp.float32)], 0)
    change = dot(sums_ref[3 * PAD :, :], weights)
    rhs = dot(basis_ref[PAD : 2 * PAD, :], traces_ref[...]) - change[3 * PAD :]
    flex_search = sums_ref[: 3 * PAD, :] - change[: 3 * PAD]
    lane = lax.broadcasted_iota(jnp.int32, (PAD, 128), 1)
    mine = (place_ref[0] * 2 + place_ref[1]) * share
    tail = jnp.zeros((PAD, 128), jnp.float32)
    for b in range(3):
        block = flex_search[b * PAD : (b + 1) * PAD]
        block = pltpu.roll(block, lax.rem(128 - mine + b * share, 128), 1)
        tail = jnp.where(lane // share == b, block, tail)
    for b in range(3):
        low = 3 * share + b * 3 * PAD
        block = sums_ref[(3 + b) * PAD : (4 + b) * PAD, :]
        block = pltpu.roll(block, (low - wide) % 128, 1)
        tail = jnp.where((lane >= low) & (lane < low + 3 * PAD), block, tail)
    sent = jnp.concatenate([rhs, tail], 0)
    for t in range(sent_ref.shape[0]):
        sent_ref[t] = sent


def order_search(own, other, place, basis, weights, subs, rows):
    count = own.shape[0]
    face = 2 * count * rows
    return pl.pallas_call(
        lambda *refs: search_kernel(count, rows, 128 // (2 * count), *refs),
        out_shape=shapes((2 * face, 128), (NEAR * PAD, 2 * face), (subs, 2 * PAD, 128)),
        in_specs=[VMEM, VMEM, SMEM, VMEM, VMEM],
        out_specs=[VMEM] * 3,
        scratch_shapes=[pltpu.VMEM((7 * PAD, 128), jnp.float32)],
        name="order_search",
    )(own, other, place, basis, weights)


def direction_kernel(subs, second_ref, near_ref, turned_ref, image_ref, search_ref, res_ref, low_ref, high_ref,
                     direction_ref, sums_ref):
    rows = res_ref.shape[0]
    rhs = jnp.concatenate(
        [second_ref[pl.ds(i, subs, stride=2 * PAD), :] for i in range(PAD)], axis=0
    )
    weights = dot(near_ref[PAD : 4 * PAD, :], rhs)
    none = jnp.zeros((128 - 6 * PAD, 128), jnp.float32)
    gap = jnp.zeros((3 * PAD, 128), jnp.float32)
    both = jnp.concatenate(
        [
            jnp.concatenate([weights, gap, none], 0),
            jnp.concatenate([gap, weights, none], 0),
        ],
        1,
    )
    change = dot(turned_ref[...], both)
    image = image_ref[...] - change[:, :128]
    direction = search_ref[...] - change[:, 128:]
    low_ref[...] = image[:rows]
    high_ref[...] = image[rows:]
    direction_ref[...] = direction[rows:]
    first = jnp.sum(res_ref[...] * search_ref[rows:, :], axis=0, keepdims=True)
    second = jnp.sum(direction * image, axis=0, keepdims=True)
    sums_ref[...] = jnp.concatenate([first, second], 0)


def project_direction(second, near, turned, image, search, res, subs):
    rows = res.shape[0]
    return pl.pallas_call(
        lambda *refs: direction_kernel(subs, *refs),
        out_shape=shapes((rows, 128), (rows, 128), (rows, 128), (2, 128)),
        in_specs=[VMEM] * 6,
        out_specs=[VMEM] * 4,
        name="project_direction",
    )(second, near, turned, image, search, res)


def moved_along(block, distance):
    n = lax.axis_size(SUB)
    return lax.ppermute(
        block, SUB, [(i - distance, i) for i in range(n) if 0 <= i - distance < n]
    )


def core_swap(block):
    return lax.ppermute(block, "c", [(0, 1), (1, 0)])


def from_all(value, axis):
    count = lax.axis_size(axis)
    return lax.all_to_all(
        jnp.broadcast_to(value[None], (count, *value.shape)), axis, 0, 0, tiled=True
    )


def along_x(piece):
    n = lax.axis_size("x")
    return [piece] + [
        lax.ppermute(piece, "x", [(i, (i + d) % n) for i in range(n)]) for d in range(1, n)
    ]


def to_all(values, axis):
    return lax.all_to_all(values, axis, 0, 0, tiled=True)


def gathered(piece):
    own = jnp.stack(along_x(piece))
    return own, core_swap(own)


def spread(part, weights):
    return lax.dot_general(
        part, weights, (((0,), (0,)), ((), ())), precision=HIGH, preferred_element_type=jnp.float32
    )


def per_device(gap, flexibility, stiffness, modes, mode_counts):
    subs = lax.axis_size(SUB)
    sub = lax.axis_index(SUB)
    place = jnp.stack([lax.axis_index("x"), lax.axis_index("c")]).astype(jnp.int32)
    rows, loads = gap.shape[1], gap.shape[2]
    lanes = lax.axis_size(IFC)
    face = rows * lanes
    mode_count = modes.shape[1]
    live = (sub < subs - 1).astype(jnp.float32)
    inner = (sub > 0).astype(jnp.float32)
    flex = flexibility.reshape(2 * rows, 2 * face)
    stiff = stiffness.reshape(2 * rows, 2 * face)

    active = (jnp.arange(PAD) < jnp.minimum(mode_counts[0], mode_count)).astype(jnp.float32)
    padded = jnp.pad(modes[0], ((0, PAD - mode_count), (0, 0), (0, 0))) * active[:, None, None]
    left, right = padded[:, 0], padded[:, 1] * live
    field = gap[0] * live

    from_before = moved_along(jnp.concatenate([field, right], 0), 1)
    left_after = moved_along(left, -1)
    field_before, right_before = from_before[:rows], from_before[rows:]
    left_in = left * inner
    piece = jnp.concatenate([-field_before, field, -right_before, left_in, right, -left_after], 0)
    none = jnp.zeros_like(left)
    own_basis = jnp.concatenate(
        [
            jnp.concatenate([-right_before, left_in, none], 0),
            jnp.concatenate([none, right, -left_after], 0),
        ],
        1,
    )
    rest = jnp.pad(
        jnp.eye(PAD, dtype=jnp.float32) * (1.0 - active)[:, None], ((0, 0), (PAD, 128 - 2 * PAD))
    )
    up, down, basis, sent = apply_stiffness(*gathered(piece), place, rest, stiff, subs)
    image, modes_image = (down[:rows], up[:rows]), (down[rows:], up[rows:])
    first = to_all(sent, SUB).reshape(subs * 2 * PAD, 128)
    before = moved_along(up, 1)
    after = moved_along(down, -1)
    top = (image[0] - before[:rows]) * inner
    bottom = (image[1] - after[:rows]) * live
    own_traces = jnp.concatenate([top, bottom], 0)
    gone = jnp.zeros((PAD, rows), jnp.float32)
    modes_top = jnp.concatenate([gone, modes_image[0], gone], 0)
    modes_top = modes_top - jnp.concatenate([before[rows:], gone, gone], 0)
    modes_bottom = jnp.concatenate([gone, modes_image[1], gone], 0)
    modes_bottom = modes_bottom - jnp.concatenate([gone, gone, after[rows:]], 0)
    own_modes = jnp.concatenate([modes_top * inner, modes_bottom * live], 1)

    flex_modes = dot_nt(basis, flex)
    small = dot_nt(flex_modes, jnp.concatenate([own_modes, own_basis], 0))
    cross = dot_nt(own_basis[PAD : 2 * PAD], own_modes)
    small = jnp.pad(small, ((0, 0), (0, 128 - small.shape[1])))
    cross = jnp.pad(cross, ((0, 0), (0, 128 - cross.shape[1])))
    piece = jnp.concatenate(
        [
            own_traces, dot(flex_modes, own_traces), small, cross, own_modes[:, :rows],
            own_modes[:, rows:],
        ],
        0,
    )
    pieces = gathered(piece)
    inverse, near, weights = coarse_inverse(sub.astype(jnp.int32)[None], first, subs, mode_count)
    search_traces, modes_traces, sent = order_search(*pieces, place, basis, weights, subs, rows)
    mine = (place[0] * 2 + place[1]) * (loads // lanes)
    share = loads // lanes
    second = to_all(sent, SUB)

    image = dot(flex, search_traces) - dot(dot_nt(flex, modes_traces), weights)
    own_search = own_traces - spread(own_modes, weights)
    own_res = field - spread(own_basis[:, rows:], weights[PAD : 4 * PAD])

    turned = jnp.concatenate([flex_modes, own_basis], 0)
    turned = jnp.pad(turned, ((0, 128 - 6 * PAD), (0, 0))).T
    low, high, direction, sums = project_direction(
        second.reshape(subs * 2 * PAD, 128), near, turned, image, own_search, own_res, subs
    )
    totals = from_all(sums, ALL).sum(0)

    low, second = lax.optimization_barrier((low, second))
    near = near[PAD : 4 * PAD]
    after = moved_along(low, -1)
    all_rhs = second[:, :PAD].transpose(1, 0, 2).reshape(PAD * subs, loads)
    my_rhs = lax.dynamic_slice_in_dim(all_rhs, mine, share, 1)
    my_weights = dot(inverse, my_rhs).reshape(PAD, subs, share).transpose(1, 0, 2)
    my_weights = jnp.pad(my_weights, ((1, 1), (0, 0), (0, 0)))
    my_weights = jnp.concatenate([my_weights[b : b + subs] for b in range(3)], 1)
    tail = second[:, PAD:]
    parts = []
    for b in range(3):
        start = 3 * share + b * 3 * PAD
        product = lax.dot_general(
            tail[:, :, start : start + 3 * PAD], my_weights, (((2,), (1,)), ((0,), (0,))),
            precision=HIGH, preferred_element_type=jnp.float32,
        )
        parts.append(tail[:, :, b * share : (b + 1) * share] - product)
    none = jnp.zeros((1, PAD, share), jnp.float32)
    last_rhs = (
        parts[1]
        + jnp.concatenate([parts[0][1:], none], 0)
        + jnp.concatenate([none, parts[2][:-1]], 0)
    )
    weights = dot(near, last_rhs.transpose(1, 0, 2).reshape(PAD * subs, share))
    weights = lax.dynamic_update_slice_in_dim(
        jnp.zeros((3 * PAD, loads), jnp.float32), weights, mine, 1
    )
    weights = weights + core_swap(weights)
    weights = sum(along_x(weights))
    own_image = (high - after) * live - spread(own_basis[:, rows:], weights)
    step = totals[0] / totals[1]
    return (step * direction)[None], (own_res - step * own_image)[None]


def solution(mesh):
    finer = Mesh(mesh.devices.reshape(8, 4, 4, 2), ALL)
    return jax.shard_map(
        per_device,
        mesh=finer,
        in_specs=(
            P(SUB, IFC, None),
            P(SUB, None, IFC, None),
            P(SUB, None, IFC, None),
            P(SUB, None, None, IFC),
            P(SUB),
        ),
        out_specs=(P(SUB, IFC, None), P(SUB, IFC, None)),
        check_vma=False,
    )
```

```python
import jax
import jax.numpy as jnp
from jax import lax
from jax.experimental import pallas as pl
from jax.experimental.pallas import tpu as pltpu
from jax.sharding import Mesh
from jax.sharding import PartitionSpec as P


SUB = ("z", "y")
IFC = ("x", "c")
ALL = SUB + IFC
HIGH = lax.Precision.HIGHEST
NEAR = 5
PAD = 8


def dot(a, b):
    return jnp.dot(a, b, precision=HIGH, preferred_element_type=jnp.float32)


def dot_nt(a, b):
    return lax.dot_general(
        a, b, (((1,), (1,)), ((), ())), precision=HIGH, preferred_element_type=jnp.float32
    )


def inverse_kernel(subs, modes, sub_ref, sent_ref, inverse_ref, near_ref, weights_ref, cols_ref):
    lanes = 128
    for i in range(PAD):
        rows = sent_ref[pl.ds(PAD + i, subs, stride=2 * PAD), :]
        turned = jnp.concatenate([rows] * (lanes // subs), axis=0).T
        cols_ref[pl.ds(i, 3 * PAD, stride=PAD), :] = turned[: 3 * PAD]

    def column(b, j):
        start = (b * PAD + j) * PAD
        return cols_ref[start : start + PAD, :]

    sublane = lax.broadcasted_iota(jnp.int32, (PAD, lanes), 0)
    lane = lax.broadcasted_iota(jnp.int32, (PAD, lanes), 1)
    lane_mode = lane // subs
    row_sub = lax.broadcasted_iota(jnp.int32, (subs, lanes), 0)
    lane_sub = lax.broadcasted_iota(jnp.int32, (subs, lanes), 1) % subs

    def inverse(a):
        a = list(a)
        for k in range(modes):
            pivot = 1.0 / a[k][k : k + 1, :]
            is_k = sublane == k
            for j in range(modes):
                if j != k:
                    scaled = a[j][k : k + 1, :] * pivot
                    a[j] = jnp.where(is_k, scaled, a[j] - a[k] * scaled)
            a[k] = jnp.where(is_k, pivot, -a[k] * pivot)
        return a

    def product(a, b):
        out = []
        for j in range(modes):
            total = a[0] * b[j][0:1, :]
            for k in range(1, modes):
                total = total + a[k] * b[j][k : k + 1, :]
            out.append(total)
        return out

    def moved(a, shift):
        return [pltpu.roll(x, shift % lanes, 1) for x in a]

    def dense(parts):
        halves = []
        for half in range(2):
            rows_of = []
            for a, shift in parts:
                chosen = jnp.zeros((PAD, lanes), jnp.float32)
                for q in range(lanes // subs):
                    k = half * (lanes // subs) + q
                    if k < modes:
                        chosen = jnp.where(lane_mode == q, a[k], chosen)
                rows_of.append((chosen, row_sub == lane_sub + shift))
            strips = []
            for i in range(PAD):
                strip = jnp.zeros((subs, lanes), jnp.float32)
                for chosen, mask in rows_of:
                    strip = jnp.where(mask, chosen[i : i + 1, :], strip)
                strips.append(strip)
            halves.append(jnp.concatenate(strips, axis=0))
        return jnp.concatenate(halves, axis=1)

    lower = [column(0, j) for j in range(modes)]
    diag = [column(1, j) for j in range(modes)]
    upper = [column(2, j) for j in range(modes)]
    ident = [jnp.where(sublane == k, 1.0, 0.0) for k in range(modes)]
    total = None
    h = 1
    while h < subs:
        inv = inverse(diag)
        alpha = product(lower, moved(inv, h))
        gamma = product(upper, moved(inv, -h))
        upper_before, lower_before = moved(upper, h), moved(lower, h)
        upper_after, lower_after = moved(upper, -h), moved(lower, -h)
        first = product(alpha, upper_before)
        second = product(gamma, lower_after)
        diag = [d - f - g for d, f, g in zip(diag, first, second)]
        lower = [-x for x in product(alpha, lower_before)]
        upper = [-x for x in product(gamma, upper_after)]
        step = dense(
            [
                (ident, 0),
                ([-x for x in moved(alpha, -h)], h),
                ([-x for x in moved(gamma, h)], -h),
            ]
        )
        total = step if total is None else dot(step, total)
        h *= 2
    whole = dot(dense([(inverse(diag), 0)]), total)
    inverse_ref[...] = whole
    row = lax.broadcasted_iota(jnp.int32, (NEAR * PAD, PAD * subs), 0)
    col = lax.broadcasted_iota(jnp.int32, (NEAR * PAD, PAD * subs), 1)
    wanted = (row % PAD) * subs + row // PAD + (sub_ref[0] - NEAR // 2)
    inside = (row // PAD + sub_ref[0] >= NEAR // 2) & (row // PAD + sub_ref[0] < subs + NEAR // 2)
    near = dot(jnp.where((col == wanted) & inside, 1.0, 0.0), whole)
    near_ref[...] = near
    rhs = jnp.concatenate(
        [sent_ref[pl.ds(i, subs, stride=2 * PAD), :] for i in range(PAD)], axis=0
    )
    weights_ref[...] = dot(near, rhs)


def coarse_inverse(sub, sent, subs, modes):
    size = subs * PAD
    vmem = pl.BlockSpec(memory_space=pltpu.VMEM)
    return pl.pallas_call(
        lambda *refs: inverse_kernel(subs, modes, *refs),
        out_shape=[
            jax.ShapeDtypeStruct((size, size), jnp.float32),
            jax.ShapeDtypeStruct((NEAR * PAD, size), jnp.float32),
            jax.ShapeDtypeStruct((NEAR * PAD, 128), jnp.float32),
        ],
        in_specs=[pl.BlockSpec(memory_space=pltpu.SMEM), vmem],
        out_specs=[vmem] * 3,
        scratch_shapes=[pltpu.VMEM((3 * PAD * PAD, 128), jnp.float32)],
        name="coarse_inverse",
    )(sub, sent)


def each_piece(count, own_ref, other_ref, place_ref, copy):
    for q in range(count):
        d = lax.rem(place_ref[0] - q + count, count)
        for c in range(2):

            @pl.when(place_ref[1] == c)
            def _():
                copy(own_ref, d, 2 * q + c)

            @pl.when(place_ref[1] != c)
            def _():
                copy(other_ref, d, 2 * q + c)


VMEM = pl.BlockSpec(memory_space=pltpu.VMEM)
SMEM = pl.BlockSpec(memory_space=pltpu.SMEM)


def shapes(*dims):
    return [jax.ShapeDtypeStruct(d, jnp.float32) for d in dims]


def stiff_kernel(count, rows, own_ref, other_ref, place_ref, rest_ref, stiff_ref, up_ref, down_ref, basis_ref,
                 sent_ref, ext_ref):
    face = 2 * count * rows
    basis_ref[2 * PAD :, :face] = jnp.zeros((PAD, face), jnp.float32)
    basis_ref[:PAD, face:] = jnp.zeros((PAD, face), jnp.float32)

    def copy(ref, d, at):
        for side in range(2):
            start = side * face + at * rows
            ext_ref[start : start + rows, :128] = ref[d, side * rows : (side + 1) * rows, :]
        lanes = slice(at * rows, (at + 1) * rows)
        basis_ref[: 2 * PAD, lanes] = ref[d, 2 * rows : 2 * rows + 2 * PAD, :]
        lanes = slice(face + at * rows, face + (at + 1) * rows)
        basis_ref[PAD:, lanes] = ref[d, 2 * rows + 2 * PAD :, :]

    each_piece(count, own_ref, other_ref, place_ref, copy)
    filler = jnp.zeros((128 - 3 * PAD, 128), jnp.float32)
    for at in range(2 * face // 128):
        lanes = slice(at * 128, (at + 1) * 128)
        ext_ref[lanes, 128:] = jnp.concatenate([basis_ref[:, lanes], filler], 0).T
    ext = ext_ref[...]
    image = 0.25 * dot(stiff_ref[...], ext)
    modes_image = image[:, 128:].T[: 3 * PAD]
    up_ref[:rows] = image[rows:, :128]
    up_ref[rows:] = modes_image[:, rows:]
    down_ref[:rows] = image[:rows, :128]
    down_ref[rows:] = modes_image[:, :rows]
    coarse = dot(basis_ref[PAD : 2 * PAD, :], ext)
    coarse = jnp.concatenate([coarse[:, :128], coarse[:, 128:] + rest_ref[...]], 0)
    for t in range(sent_ref.shape[0]):
        sent_ref[t] = coarse


def apply_stiffness(own, other, place, rest, stiff, subs):
    count, rows = own.shape[0], stiff.shape[0] // 2
    face = 2 * count * rows
    return pl.pallas_call(
        lambda *refs: stiff_kernel(count, rows, *refs),
        out_shape=shapes(
            (rows + 3 * PAD, 128), (rows + 3 * PAD, 128), (3 * PAD, 2 * face), (subs, 2 * PAD, 128)
        ),
        in_specs=[VMEM, VMEM, SMEM, VMEM, VMEM],
        out_specs=[VMEM] * 4,
        scratch_shapes=[pltpu.VMEM((2 * face, 256), jnp.float32)],
        name="apply_stiffness",
    )(own, other, place, rest, stiff)


def search_kernel(count, rows, share, own_ref, other_ref, place_ref, basis_ref, weights_ref, traces_ref,
                  modes_ref, sent_ref, sums_ref):
    face = 2 * count * rows
    wide = NEAR * PAD
    head = 2 * rows
    sums_ref[...] = own_ref[0, head : head + 7 * PAD, :] + other_ref[0, head : head + 7 * PAD, :]
    for d in range(1, count):
        sums_ref[...] += own_ref[d, head : head + 7 * PAD, :] + other_ref[d, head : head + 7 * PAD, :]

    def copy(ref, d, at):
        for side in range(2):
            start = side * face + at * rows
            traces_ref[start : start + rows, :] = ref[d, side * rows : (side + 1) * rows, :]
            low = head + 7 * PAD + side * wide
            modes_ref[:, start : start + rows] = ref[d, low : low + wide, :]

    each_piece(count, own_ref, other_ref, place_ref, copy)
    weights = jnp.concatenate([weights_ref[...], jnp.zeros((128 - wide, 128), jnp.float32)], 0)
    change = dot(sums_ref[3 * PAD :, :], weights)
    rhs = dot(basis_ref[PAD : 2 * PAD, :], traces_ref[...]) - change[3 * PAD :]
    flex_search = sums_ref[: 3 * PAD, :] - change[: 3 * PAD]
    lane = lax.broadcasted_iota(jnp.int32, (PAD, 128), 1)
    mine = (place_ref[0] * 2 + place_ref[1]) * share
    tail = jnp.zeros((PAD, 128), jnp.float32)
    for b in range(3):
        block = flex_search[b * PAD : (b + 1) * PAD]
        block = pltpu.roll(block, lax.rem(128 - mine + b * share, 128), 1)
        tail = jnp.where(lane // share == b, block, tail)
    for b in range(3):
        low = 3 * share + b * 3 * PAD
        block = sums_ref[(3 + b) * PAD : (4 + b) * PAD, :]
        block = pltpu.roll(block, (low - wide) % 128, 1)
        tail = jnp.where((lane >= low) & (lane < low + 3 * PAD), block, tail)
    sent = jnp.concatenate([rhs, tail], 0)
    for t in range(sent_ref.shape[0]):
        sent_ref[t] = sent


def order_search(own, other, place, basis, weights, subs, rows):
    count = own.shape[0]
    face = 2 * count * rows
    return pl.pallas_call(
        lambda *refs: search_kernel(count, rows, 128 // (2 * count), *refs),
        out_shape=shapes((2 * face, 128), (NEAR * PAD, 2 * face), (subs, 2 * PAD, 128)),
        in_specs=[VMEM, VMEM, SMEM, VMEM, VMEM],
        out_specs=[VMEM] * 3,
        scratch_shapes=[pltpu.VMEM((7 * PAD, 128), jnp.float32)],
        name="order_search",
    )(own, other, place, basis, weights)


def direction_kernel(subs, second_ref, near_ref, turned_ref, image_ref, search_ref, res_ref, low_ref, high_ref,
                     direction_ref, sums_ref):
    rows = res_ref.shape[0]
    rhs = jnp.concatenate(
        [second_ref[pl.ds(i, subs, stride=2 * PAD), :] for i in range(PAD)], axis=0
    )
    weights = dot(near_ref[PAD : 4 * PAD, :], rhs)
    none = jnp.zeros((128 - 6 * PAD, 128), jnp.float32)
    gap = jnp.zeros((3 * PAD, 128), jnp.float32)
    both = jnp.concatenate(
        [
            jnp.concatenate([weights, gap, none], 0),
            jnp.concatenate([gap, weights, none], 0),
        ],
        1,
    )
    change = dot(turned_ref[...], both)
    image = image_ref[...] - change[:, :128]
    direction = search_ref[...] - change[:, 128:]
    low_ref[...] = image[:rows]
    high_ref[...] = image[rows:]
    direction_ref[...] = direction[rows:]
    first = jnp.sum(res_ref[...] * search_ref[rows:, :], axis=0, keepdims=True)
    second = jnp.sum(direction * image, axis=0, keepdims=True)
    sums_ref[...] = jnp.concatenate([first, second], 0)


def project_direction(second, near, turned, image, search, res, subs):
    rows = res.shape[0]
    return pl.pallas_call(
        lambda *refs: direction_kernel(subs, *refs),
        out_shape=shapes((rows, 128), (rows, 128), (rows, 128), (2, 128)),
        in_specs=[VMEM] * 6,
        out_specs=[VMEM] * 4,
        name="project_direction",
    )(second, near, turned, image, search, res)


def result_kernel(totals_ref, direction_ref, res_ref, high_ref, after_ref, turned_ref, live_ref, *refs):
    parts, (multipliers_ref, residual_ref) = refs[:-2], refs[-2:]
    weights = parts[0][...]
    for part in parts[1:]:
        weights = weights + part[...]
    rows = res_ref.shape[0]
    gap = jnp.zeros((3 * PAD, 128), jnp.float32)
    none = jnp.zeros((128 - 6 * PAD, 128), jnp.float32)
    change = dot(turned_ref[rows:, :], jnp.concatenate([gap, weights, none], 0))
    step = totals_ref[0:1, :] / totals_ref[1:2, :]
    image = (high_ref[...] - after_ref[...]) * live_ref[0] - change
    multipliers_ref[0] = step * direction_ref[...]
    residual_ref[0] = res_ref[...] - step * image


def results(totals, direction, res, high, after, turned, live, parts):
    return pl.pallas_call(
        result_kernel,
        out_shape=shapes((1, *res.shape), (1, *res.shape)),
        in_specs=[VMEM] * 6 + [SMEM] + [VMEM] * len(parts),
        out_specs=[VMEM] * 2,
        name="results",
    )(totals, direction, res, high, after, turned, live[None], *parts)


def moved_along(block, distance):
    n = lax.axis_size(SUB)
    return lax.ppermute(
        block, SUB, [(i - distance, i) for i in range(n) if 0 <= i - distance < n]
    )


def core_swap(block):
    return lax.ppermute(block, "c", [(0, 1), (1, 0)])


def from_all(value, axis):
    count = lax.axis_size(axis)
    return lax.all_to_all(
        jnp.broadcast_to(value[None], (count, *value.shape)), axis, 0, 0, tiled=True
    )


def along_x(piece):
    n = lax.axis_size("x")
    return [piece] + [
        lax.ppermute(piece, "x", [(i, (i + d) % n) for i in range(n)]) for d in range(1, n)
    ]


def to_all(values, axis):
    return lax.all_to_all(values, axis, 0, 0, tiled=True)


def gathered(piece):
    pieces = along_x(piece)
    own = jnp.stack(pieces)
    return own, core_swap(own)


def spread(part, weights):
    return lax.dot_general(
        part, weights, (((0,), (0,)), ((), ())), precision=HIGH, preferred_element_type=jnp.float32
    )


def per_device(gap, flexibility, stiffness, modes, mode_counts):
    subs = lax.axis_size(SUB)
    sub = lax.axis_index(SUB)
    place = jnp.stack([lax.axis_index("x"), lax.axis_index("c")]).astype(jnp.int32)
    rows, loads = gap.shape[1], gap.shape[2]
    lanes = lax.axis_size(IFC)
    face = rows * lanes
    mode_count = modes.shape[1]
    live = (sub < subs - 1).astype(jnp.float32)
    inner = (sub > 0).astype(jnp.float32)
    flex = flexibility.reshape(2 * rows, 2 * face)
    stiff = stiffness.reshape(2 * rows, 2 * face)

    active = (jnp.arange(PAD) < jnp.minimum(mode_counts[0], mode_count)).astype(jnp.float32)
    padded = jnp.pad(modes[0], ((0, PAD - mode_count), (0, 0), (0, 0))) * active[:, None, None]
    left, right = padded[:, 0], padded[:, 1] * live
    field = gap[0] * live

    from_before = moved_along(jnp.concatenate([field, right], 0), 1)
    left_after = moved_along(left, -1)
    field_before, right_before = from_before[:rows], from_before[rows:]
    left_in = left * inner
    piece = jnp.concatenate([-field_before, field, -right_before, left_in, right, -left_after], 0)
    none = jnp.zeros_like(left)
    own_basis = jnp.concatenate(
        [
            jnp.concatenate([-right_before, left_in, none], 0),
            jnp.concatenate([none, right, -left_after], 0),
        ],
        1,
    )
    rest = jnp.pad(
        jnp.eye(PAD, dtype=jnp.float32) * (1.0 - active)[:, None], ((0, 0), (PAD, 128 - 2 * PAD))
    )
    up, down, basis, sent = apply_stiffness(*gathered(piece), place, rest, stiff, subs)
    image, modes_image = (down[:rows], up[:rows]), (down[rows:], up[rows:])
    first = to_all(sent, SUB).reshape(subs * 2 * PAD, 128)
    before = moved_along(up, 1)
    after = moved_along(down, -1)
    top = (image[0] - before[:rows]) * inner
    bottom = (image[1] - after[:rows]) * live
    own_traces = jnp.concatenate([top, bottom], 0)
    gone = jnp.zeros((PAD, rows), jnp.float32)
    modes_top = jnp.concatenate([gone, modes_image[0], gone], 0)
    modes_top = modes_top - jnp.concatenate([before[rows:], gone, gone], 0)
    modes_bottom = jnp.concatenate([gone, modes_image[1], gone], 0)
    modes_bottom = modes_bottom - jnp.concatenate([gone, gone, after[rows:]], 0)
    own_modes = jnp.concatenate([modes_top * inner, modes_bottom * live], 1)

    flex_modes = dot_nt(basis, flex)
    small = dot_nt(flex_modes, jnp.concatenate([own_modes, own_basis], 0))
    cross = dot_nt(own_basis[PAD : 2 * PAD], own_modes)
    small = jnp.pad(small, ((0, 0), (0, 128 - small.shape[1])))
    cross = jnp.pad(cross, ((0, 0), (0, 128 - cross.shape[1])))
    piece = jnp.concatenate(
        [
            own_traces, dot(flex_modes, own_traces), small, cross, own_modes[:, :rows],
            own_modes[:, rows:],
        ],
        0,
    )
    pieces = gathered(piece)
    inverse, near, weights = coarse_inverse(sub.astype(jnp.int32)[None], first, subs, mode_count)
    search_traces, modes_traces, sent = order_search(*pieces, place, basis, weights, subs, rows)
    mine = (place[0] * 2 + place[1]) * (loads // lanes)
    share = loads // lanes
    second = to_all(sent, SUB)

    image = dot(flex, search_traces) - dot(dot_nt(flex, modes_traces), weights)
    own_search = own_traces - spread(own_modes, weights)
    own_res = field - spread(own_basis[:, rows:], weights[PAD : 4 * PAD])
    turned = jnp.concatenate([flex_modes, own_basis], 0)
    turned = jnp.pad(turned, ((0, 128 - 6 * PAD), (0, 0))).T
    low, high, direction, sums = project_direction(
        second.reshape(subs * 2 * PAD, 128), near, turned, image, own_search, own_res, subs
    )
    totals = from_all(sums, ALL)
    totals = totals.sum(0)

    after = moved_along(low, -1)
    near = near[PAD : 4 * PAD]
    all_rhs = second[:, :PAD].transpose(1, 0, 2).reshape(PAD * subs, loads)
    my_rhs = lax.dynamic_slice_in_dim(all_rhs, mine, share, 1)
    my_weights = dot(inverse, my_rhs).reshape(PAD, subs, share).transpose(1, 0, 2)
    my_weights = jnp.pad(my_weights, ((1, 1), (0, 0), (0, 0)))
    my_weights = jnp.concatenate([my_weights[b : b + subs] for b in range(3)], 1)
    tail = second[:, PAD:]
    parts = []
    for b in range(3):
        start = 3 * share + b * 3 * PAD
        product = lax.dot_general(
            tail[:, :, start : start + 3 * PAD], my_weights, (((2,), (1,)), ((0,), (0,))),
            precision=HIGH, preferred_element_type=jnp.float32,
        )
        parts.append(tail[:, :, b * share : (b + 1) * share] - product)
    none = jnp.zeros((1, PAD, share), jnp.float32)
    last_rhs = (
        parts[1]
        + jnp.concatenate([parts[0][1:], none], 0)
        + jnp.concatenate([none, parts[2][:-1]], 0)
    )
    weights = dot(near, last_rhs.transpose(1, 0, 2).reshape(PAD * subs, share))
    weights = lax.dynamic_update_slice_in_dim(
        jnp.zeros((3 * PAD, loads), jnp.float32), weights, mine, 1
    )
    weights = weights + core_swap(weights)
    return results(totals, direction, own_res, high, after, turned, live, along_x(weights))


def solution(mesh):
    finer = Mesh(mesh.devices.reshape(8, 4, 4, 2), ALL)
    return jax.shard_map(
        per_device,
        mesh=finer,
        in_specs=(
            P(SUB, IFC, None),
            P(SUB, None, IFC, None),
            P(SUB, None, IFC, None),
            P(SUB, None, None, IFC),
            P(SUB),
        ),
        out_specs=(P(SUB, IFC, None), P(SUB, IFC, None)),
        check_vma=False,
    )
```

```python
import jax
import jax.numpy as jnp
from jax import lax
from jax.experimental import pallas as pl
from jax.experimental.pallas import tpu as pltpu
from jax.sharding import Mesh
from jax.sharding import PartitionSpec as P


SUB = ("z", "y")
IFC = ("x", "c")
ALL = SUB + IFC
HIGH = lax.Precision.HIGHEST
NEAR = 5
PAD = 8


def dot(a, b):
    return jnp.dot(a, b, precision=HIGH, preferred_element_type=jnp.float32)


def dot_nt(a, b):
    return lax.dot_general(
        a, b, (((1,), (1,)), ((), ())), precision=HIGH, preferred_element_type=jnp.float32
    )


def inverse_kernel(subs, modes, sub_ref, sent_ref, inverse_ref, near_ref, weights_ref, cols_ref):
    lanes = 128
    for i in range(PAD):
        rows = sent_ref[pl.ds(PAD + i, subs, stride=2 * PAD), :]
        turned = jnp.concatenate([rows] * (lanes // subs), axis=0).T
        cols_ref[pl.ds(i, 3 * PAD, stride=PAD), :] = turned[: 3 * PAD]

    def column(b, j):
        start = (b * PAD + j) * PAD
        return cols_ref[start : start + PAD, :]

    sublane = lax.broadcasted_iota(jnp.int32, (PAD, lanes), 0)
    lane = lax.broadcasted_iota(jnp.int32, (PAD, lanes), 1)
    lane_mode = lane // subs
    row_sub = lax.broadcasted_iota(jnp.int32, (subs, lanes), 0)
    lane_sub = lax.broadcasted_iota(jnp.int32, (subs, lanes), 1) % subs

    def inverse(a):
        a = list(a)
        for k in range(modes):
            pivot = 1.0 / a[k][k : k + 1, :]
            is_k = sublane == k
            for j in range(modes):
                if j != k:
                    scaled = a[j][k : k + 1, :] * pivot
                    a[j] = jnp.where(is_k, scaled, a[j] - a[k] * scaled)
            a[k] = jnp.where(is_k, pivot, -a[k] * pivot)
        return a

    def product(a, b):
        out = []
        for j in range(modes):
            total = a[0] * b[j][0:1, :]
            for k in range(1, modes):
                total = total + a[k] * b[j][k : k + 1, :]
            out.append(total)
        return out

    def moved(a, shift):
        return [pltpu.roll(x, shift % lanes, 1) for x in a]

    def dense(parts):
        halves = []
        for half in range(2):
            rows_of = []
            for a, shift in parts:
                chosen = jnp.zeros((PAD, lanes), jnp.float32)
                for q in range(lanes // subs):
                    k = half * (lanes // subs) + q
                    if k < modes:
                        chosen = jnp.where(lane_mode == q, a[k], chosen)
                rows_of.append((chosen, row_sub == lane_sub + shift))
            strips = []
            for i in range(PAD):
                strip = jnp.zeros((subs, lanes), jnp.float32)
                for chosen, mask in rows_of:
                    strip = jnp.where(mask, chosen[i : i + 1, :], strip)
                strips.append(strip)
            halves.append(jnp.concatenate(strips, axis=0))
        return jnp.concatenate(halves, axis=1)

    lower = [column(0, j) for j in range(modes)]
    diag = [column(1, j) for j in range(modes)]
    upper = [column(2, j) for j in range(modes)]
    ident = [jnp.where(sublane == k, 1.0, 0.0) for k in range(modes)]
    total = None
    h = 1
    while h < subs:
        inv = inverse(diag)
        alpha = product(lower, moved(inv, h))
        gamma = product(upper, moved(inv, -h))
        upper_before, lower_before = moved(upper, h), moved(lower, h)
        upper_after, lower_after = moved(upper, -h), moved(lower, -h)
        first = product(alpha, upper_before)
        second = product(gamma, lower_after)
        diag = [d - f - g for d, f, g in zip(diag, first, second)]
        lower = [-x for x in product(alpha, lower_before)]
        upper = [-x for x in product(gamma, upper_after)]
        step = dense(
            [
                (ident, 0),
                ([-x for x in moved(alpha, -h)], h),
                ([-x for x in moved(gamma, h)], -h),
            ]
        )
        total = step if total is None else dot(step, total)
        h *= 2
    whole = dot(dense([(inverse(diag), 0)]), total)
    inverse_ref[...] = whole
    row = lax.broadcasted_iota(jnp.int32, (NEAR * PAD, PAD * subs), 0)
    col = lax.broadcasted_iota(jnp.int32, (NEAR * PAD, PAD * subs), 1)
    wanted = (row % PAD) * subs + row // PAD + (sub_ref[0] - NEAR // 2)
    inside = (row // PAD + sub_ref[0] >= NEAR // 2) & (row // PAD + sub_ref[0] < subs + NEAR // 2)
    near = dot(jnp.where((col == wanted) & inside, 1.0, 0.0), whole)
    near_ref[...] = near
    rhs = jnp.concatenate(
        [sent_ref[pl.ds(i, subs, stride=2 * PAD), :] for i in range(PAD)], axis=0
    )
    weights_ref[...] = dot(near, rhs)


def coarse_inverse(sub, sent, subs, modes):
    size = subs * PAD
    vmem = pl.BlockSpec(memory_space=pltpu.VMEM)
    return pl.pallas_call(
        lambda *refs: inverse_kernel(subs, modes, *refs),
        out_shape=[
            jax.ShapeDtypeStruct((size, size), jnp.float32),
            jax.ShapeDtypeStruct((NEAR * PAD, size), jnp.float32),
            jax.ShapeDtypeStruct((NEAR * PAD, 128), jnp.float32),
        ],
        in_specs=[pl.BlockSpec(memory_space=pltpu.SMEM), vmem],
        out_specs=[vmem] * 3,
        scratch_shapes=[pltpu.VMEM((3 * PAD * PAD, 128), jnp.float32)],
        name="coarse_inverse",
    )(sub, sent)


def each_piece(pieces, place_ref, copy):
    count = len(pieces) // 2
    for d in range(count):
        q = lax.rem(place_ref[0] - d + count, count)
        copy(pieces[d], 2 * q + place_ref[1])
        copy(pieces[count + d], 2 * q + 1 - place_ref[1])


def dot3(a, b):
    a_high, b_high = a.astype(jnp.bfloat16), b.astype(jnp.bfloat16)
    a_low = (a - a_high.astype(jnp.float32)).astype(jnp.bfloat16)
    b_low = (b - b_high.astype(jnp.float32)).astype(jnp.bfloat16)

    def part(x, y):
        return jnp.dot(x, y, preferred_element_type=jnp.float32)

    return part(a_high, b_high) + (part(a_high, b_low) + part(a_low, b_high))


def turned_into(ext_ref, rows_ref, count):
    filler = jnp.zeros((128 - rows_ref.shape[0], 128), jnp.float32)
    for at in range(count):
        lanes = slice(at * 128, (at + 1) * 128)
        ext_ref[lanes, 128:] = jnp.concatenate([rows_ref[:, lanes], filler], 0).T


VMEM = pl.BlockSpec(memory_space=pltpu.VMEM)
SMEM = pl.BlockSpec(memory_space=pltpu.SMEM)


def shapes(*dims):
    return [jax.ShapeDtypeStruct(d, jnp.float32) for d in dims]


def stiff_kernel(rows, count, *refs):
    pieces, refs = refs[: 2 * count], refs[2 * count :]
    place_ref, rest_ref, stiff_ref, up_ref, down_ref, image_ref, basis_ref, sent_ref, ext_ref = refs
    face = 2 * count * rows
    basis_ref[2 * PAD :, :face] = jnp.zeros((PAD, face), jnp.float32)
    basis_ref[:PAD, face:] = jnp.zeros((PAD, face), jnp.float32)

    def copy(ref, at):
        for side in range(2):
            start = pl.multiple_of(side * face + at * rows, rows)
            ext_ref[pl.ds(start, rows), :128] = ref[side * rows : (side + 1) * rows, :]
        lanes = pl.ds(pl.multiple_of(at * rows, rows), rows)
        basis_ref[: 2 * PAD, lanes] = ref[2 * rows : 2 * rows + 2 * PAD, :]
        lanes = pl.ds(pl.multiple_of(face + at * rows, rows), rows)
        basis_ref[PAD:, lanes] = ref[2 * rows + 2 * PAD :, :]

    each_piece(pieces, place_ref, copy)
    turned_into(ext_ref, basis_ref, 2 * face // 128)
    ext = ext_ref[...]
    image = 0.25 * dot3(stiff_ref[...], ext)
    modes_image = image[:, 128:].T[: 3 * PAD]
    up_ref[:rows] = image[rows:, :128]
    up_ref[rows:] = modes_image[:, rows:]
    down_ref[:rows] = image[:rows, :128]
    down_ref[rows:] = modes_image[:, :rows]
    image_ref[...] = modes_image
    coarse = dot(basis_ref[PAD : 2 * PAD, :], ext)
    coarse = jnp.concatenate([coarse[:, :128], coarse[:, 128:] + rest_ref[...]], 0)
    for t in range(sent_ref.shape[0]):
        sent_ref[t] = coarse


def apply_stiffness(pieces, place, rest, stiff, subs):
    rows, face = stiff.shape[0] // 2, stiff.shape[1] // 2
    return pl.pallas_call(
        lambda *refs: stiff_kernel(rows, len(pieces) // 2, *refs),
        out_shape=shapes(
            (rows + 3 * PAD, 128), (rows + 3 * PAD, 128), (3 * PAD, 2 * rows), (3 * PAD, 2 * face),
            (subs, 2 * PAD, 128),
        ),
        in_specs=[VMEM] * len(pieces) + [SMEM, VMEM, VMEM],
        out_specs=[VMEM] * 5,
        scratch_shapes=[pltpu.VMEM((2 * face, 256), jnp.float32)],
        name="apply_stiffness",
    )(*pieces, place, rest, stiff)


def search_kernel(rows, count, share, *refs):
    pieces, refs = refs[: 2 * count], refs[2 * count :]
    place_ref, basis_ref, weights_ref, traces_ref, modes_ref, sent_ref = refs
    face = 2 * count * rows
    wide = NEAR * PAD
    head = 2 * rows
    sums = pieces[0][head : head + 7 * PAD, :]
    for ref in pieces[1:]:
        sums = sums + ref[head : head + 7 * PAD, :]

    def copy(ref, at):
        for side in range(2):
            at_rows = pl.ds(pl.multiple_of(side * face + at * rows, rows), rows)
            traces_ref[at_rows, :] = ref[side * rows : (side + 1) * rows, :]
            low = head + 7 * PAD + side * wide
            modes_ref[:, at_rows] = ref[low : low + wide, :]

    each_piece(pieces, place_ref, copy)
    weights = jnp.concatenate([weights_ref[...], jnp.zeros((128 - wide, 128), jnp.float32)], 0)
    change = dot(sums[3 * PAD :], weights)
    rhs = dot(basis_ref[PAD : 2 * PAD, :], traces_ref[...]) - change[3 * PAD :]
    flex_search = sums[: 3 * PAD] - change[: 3 * PAD]
    lane = lax.broadcasted_iota(jnp.int32, (PAD, 128), 1)
    mine = (place_ref[0] * 2 + place_ref[1]) * share
    tail = jnp.zeros((PAD, 128), jnp.float32)
    for b in range(3):
        block = flex_search[b * PAD : (b + 1) * PAD]
        block = pltpu.roll(block, lax.rem(128 - mine + b * share, 128), 1)
        tail = jnp.where(lane // share == b, block, tail)
    for b in range(3):
        low = 3 * share + b * 3 * PAD
        block = pltpu.roll(sums[(3 + b) * PAD : (4 + b) * PAD], (low - wide) % 128, 1)
        tail = jnp.where((lane >= low) & (lane < low + 3 * PAD), block, tail)
    sent = jnp.concatenate([rhs, tail], 0)
    for t in range(sent_ref.shape[0]):
        sent_ref[t] = sent


def order_search(pieces, place, basis, weights, subs, rows):
    face = len(pieces) * rows
    return pl.pallas_call(
        lambda *refs: search_kernel(rows, len(pieces) // 2, 128 // len(pieces), *refs),
        out_shape=shapes((2 * face, 128), (NEAR * PAD, 2 * face), (subs, 2 * PAD, 128)),
        in_specs=[VMEM] * len(pieces) + [SMEM, VMEM, VMEM],
        out_specs=[VMEM] * 3,
        name="order_search",
    )(*pieces, place, basis, weights)


def flex_kernel(flex_ref, traces_ref, modes_ref, weights_ref, own_ref, own_modes_ref, field_ref, own_basis_ref,
                flex_modes_ref, image_ref, search_ref, res_ref, turned_ref, ext_ref):
    rows = field_ref.shape[0]
    wide = NEAR * PAD
    weights = jnp.concatenate([weights_ref[...], jnp.zeros((128 - wide, 128), jnp.float32)], 0)
    ext_ref[:, :128] = traces_ref[...]
    turned_into(ext_ref, modes_ref, traces_ref.shape[0] // 128)
    both = dot3(flex_ref[...], ext_ref[...])
    image_ref[...] = both[:, :128] - dot(both[:, 128:], weights)
    own_modes = jnp.concatenate(
        [own_modes_ref[...], jnp.zeros((128 - wide, 2 * rows), jnp.float32)], 0
    ).T
    search_ref[...] = own_ref[...] - dot(own_modes, weights)
    turned = jnp.concatenate(
        [
            flex_modes_ref[...], own_basis_ref[...],
            jnp.zeros((128 - 6 * PAD, 2 * rows), jnp.float32),
        ],
        0,
    ).T
    turned_ref[...] = turned
    gap = jnp.zeros((3 * PAD, 128), jnp.float32)
    none = jnp.zeros((128 - 6 * PAD, 128), jnp.float32)
    shifted = jnp.concatenate([gap, weights_ref[PAD : 4 * PAD, :], none], 0)
    res_ref[...] = field_ref[...] - dot(turned[rows:], shifted)


def apply_flexibility(flex, traces, modes, weights, own, own_modes, field, own_basis, flex_modes):
    rows = field.shape[0]
    return pl.pallas_call(
        flex_kernel,
        out_shape=shapes((2 * rows, 128), (2 * rows, 128), (rows, 128), (2 * rows, 128)),
        in_specs=[VMEM] * 9,
        out_specs=[VMEM] * 4,
        scratch_shapes=[pltpu.VMEM((traces.shape[0], 256), jnp.float32)],
        name="apply_flexibility",
    )(flex, traces, modes, weights, own, own_modes, field, own_basis, flex_modes)


def last_kernel(subs, modes, share, place_ref, second_ref, inverse_ref, near_ref, out_ref):
    mine = (place_ref[0] * 2 + place_ref[1]) * share
    lane = lax.broadcasted_iota(jnp.int32, (subs, 128), 1)
    row = lax.broadcasted_iota(jnp.int32, (subs, 128), 0)
    rhs = jnp.concatenate(
        [second_ref[pl.ds(i, subs, stride=2 * PAD), :] for i in range(PAD)], axis=0
    )
    weights = dot(inverse_ref[...], pltpu.roll(rhs, lax.rem(128 - mine, 128), 1))

    def earlier(x):
        return jnp.where(row == 0, 0.0, pltpu.roll(x, 1, 0))

    def later(x):
        return jnp.where(row == subs - 1, 0.0, pltpu.roll(x, subs - 1, 0))

    near = []
    for k in range(modes):
        here = weights[k * subs : (k + 1) * subs]
        near.append((earlier(here), here, later(here)))
    out = []
    for i in range(PAD):
        tail = second_ref[pl.ds(PAD + i, subs, stride=2 * PAD), :]
        parts = []
        for b in range(3):
            part = tail if b == 0 else pltpu.roll(tail, 128 - b * share, 1)
            if i < modes:
                for c in range(3):
                    for k in range(modes):
                        at = 3 * share + b * 3 * PAD + c * PAD + k
                        part = part - tail[:, at : at + 1] * near[k][c]
            parts.append(part)
        total = parts[1] + later(parts[0]) + earlier(parts[2])
        out.append(jnp.where(lane < share, total, 0.0))
    last = dot(near_ref[PAD : 4 * PAD, :], jnp.concatenate(out, 0))
    out_ref[...] = pltpu.roll(last, mine, 1)


def last_weights(place, second, inverse, near, subs, modes, share):
    return pl.pallas_call(
        lambda *refs: last_kernel(subs, modes, share, *refs),
        out_shape=shapes((3 * PAD, 128))[0],
        in_specs=[SMEM] + [VMEM] * 3,
        out_specs=VMEM,
        name="last_weights",
    )(place, second, inverse, near)


def direction_kernel(subs, second_ref, near_ref, turned_ref, image_ref, search_ref, res_ref, low_ref, high_ref,
                     direction_ref, sums_ref):
    rows = res_ref.shape[0]
    rhs = jnp.concatenate(
        [second_ref[pl.ds(i, subs, stride=2 * PAD), :] for i in range(PAD)], axis=0
    )
    weights = dot(near_ref[PAD : 4 * PAD, :], rhs)
    none = jnp.zeros((128 - 6 * PAD, 128), jnp.float32)
    gap = jnp.zeros((3 * PAD, 128), jnp.float32)
    both = jnp.concatenate(
        [
            jnp.concatenate([weights, gap, none], 0),
            jnp.concatenate([gap, weights, none], 0),
        ],
        1,
    )
    change = dot(turned_ref[...], both)
    image = image_ref[...] - change[:, :128]
    direction = search_ref[...] - change[:, 128:]
    low_ref[...] = image[:rows]
    high_ref[...] = image[rows:]
    direction_ref[...] = direction[rows:]
    first = jnp.sum(res_ref[...] * search_ref[rows:, :], axis=0, keepdims=True)
    second = jnp.sum(direction * image, axis=0, keepdims=True)
    sums_ref[...] = jnp.concatenate([first, second], 0)


def project_direction(second, near, turned, image, search, res, subs):
    rows = res.shape[0]
    return pl.pallas_call(
        lambda *refs: direction_kernel(subs, *refs),
        out_shape=shapes((rows, 128), (rows, 128), (rows, 128), (2, 128)),
        in_specs=[VMEM] * 6,
        out_specs=[VMEM] * 4,
        name="project_direction",
    )(second, near, turned, image, search, res)


def result_kernel(totals_ref, direction_ref, res_ref, high_ref, after_ref, turned_ref, live_ref, *refs):
    parts, (multipliers_ref, residual_ref) = refs[:-2], refs[-2:]
    weights = parts[0][...]
    for part in parts[1:]:
        weights = weights + part[...]
    rows = res_ref.shape[0]
    gap = jnp.zeros((3 * PAD, 128), jnp.float32)
    none = jnp.zeros((128 - 6 * PAD, 128), jnp.float32)
    change = dot(turned_ref[rows:, :], jnp.concatenate([gap, weights, none], 0))
    step = totals_ref[0:1, :] / totals_ref[1:2, :]
    image = (high_ref[...] - after_ref[...]) * live_ref[0] - change
    multipliers_ref[0] = step * direction_ref[...]
    residual_ref[0] = res_ref[...] - step * image


def results(totals, direction, res, high, after, turned, live, parts):
    return pl.pallas_call(
        result_kernel,
        out_shape=shapes((1, *res.shape), (1, *res.shape)),
        in_specs=[VMEM] * 6 + [SMEM] + [VMEM] * len(parts),
        out_specs=[VMEM] * 2,
        name="results",
    )(totals, direction, res, high, after, turned, live[None], *parts)


def moved_along(block, distance):
    n = lax.axis_size(SUB)
    return lax.ppermute(
        block, SUB, [(i - distance, i) for i in range(n) if 0 <= i - distance < n]
    )


def core_swap(block):
    return lax.ppermute(block, "c", [(0, 1), (1, 0)])


def from_all(value, axis):
    count = lax.axis_size(axis)
    return lax.all_to_all(
        jnp.broadcast_to(value[None], (count, *value.shape)), axis, 0, 0, tiled=True
    )


def along_x(piece):
    n = lax.axis_size("x")
    return [piece] + [
        lax.ppermute(piece, "x", [(i, (i + d) % n) for i in range(n)]) for d in range(1, n)
    ]


def to_all(values, axis):
    return lax.all_to_all(values, axis, 0, 0, tiled=True)


def gathered(piece):
    pieces = along_x(piece)
    return pieces + [core_swap(part) for part in pieces]


def per_device(gap, flexibility, stiffness, modes, mode_counts):
    subs = lax.axis_size(SUB)
    sub = lax.axis_index(SUB)
    place = jnp.stack([lax.axis_index("x"), lax.axis_index("c")]).astype(jnp.int32)
    rows, loads = gap.shape[1], gap.shape[2]
    lanes = lax.axis_size(IFC)
    face = rows * lanes
    mode_count = modes.shape[1]
    live = (sub < subs - 1).astype(jnp.float32)
    inner = (sub > 0).astype(jnp.float32)
    flex = flexibility.reshape(2 * rows, 2 * face)
    stiff = stiffness.reshape(2 * rows, 2 * face)

    active = (jnp.arange(PAD) < jnp.minimum(mode_counts[0], mode_count)).astype(jnp.float32)
    padded = jnp.pad(modes[0], ((0, PAD - mode_count), (0, 0), (0, 0))) * active[:, None, None]
    left, right = padded[:, 0], padded[:, 1] * live
    field = gap[0] * live

    from_before = moved_along(jnp.concatenate([field, right], 0), 1)
    left_after = moved_along(left, -1)
    field_before, right_before = from_before[:rows], from_before[rows:]
    left_in = left * inner
    piece = jnp.concatenate([-field_before, field, -right_before, left_in, right, -left_after], 0)
    none = jnp.zeros_like(left)
    own_basis = jnp.concatenate(
        [
            jnp.concatenate([-right_before, left_in, none], 0),
            jnp.concatenate([none, right, -left_after], 0),
        ],
        1,
    )
    rest = jnp.pad(
        jnp.eye(PAD, dtype=jnp.float32) * (1.0 - active)[:, None], ((0, 0), (PAD, 128 - 2 * PAD))
    )
    up, down, modes_image, basis, sent = apply_stiffness(gathered(piece), place, rest, stiff, subs)
    first = to_all(sent, SUB).reshape(subs * 2 * PAD, 128)
    before = moved_along(up, 1)
    after = moved_along(down, -1)
    top = (down[:rows] - before[:rows]) * inner
    bottom = (up[:rows] - after[:rows]) * live
    own_traces = jnp.concatenate([top, bottom], 0)
    gone = jnp.zeros((PAD, rows), jnp.float32)
    modes_top = jnp.concatenate([gone, modes_image[:, :rows], gone], 0)
    modes_top = modes_top - jnp.concatenate([before[rows:], gone, gone], 0)
    modes_bottom = jnp.concatenate([gone, modes_image[:, rows:], gone], 0)
    modes_bottom = modes_bottom - jnp.concatenate([gone, gone, after[rows:]], 0)
    own_modes = jnp.concatenate([modes_top * inner, modes_bottom * live], 1)

    flex_modes = dot_nt(basis, flex)
    small = dot_nt(flex_modes, jnp.concatenate([own_modes, own_basis], 0))
    cross = dot_nt(own_basis[PAD : 2 * PAD], own_modes)
    small = jnp.pad(small, ((0, 0), (0, 128 - small.shape[1])))
    cross = jnp.pad(cross, ((0, 0), (0, 128 - cross.shape[1])))
    piece = jnp.concatenate(
        [
            own_traces, dot(flex_modes, own_traces), small, cross, own_modes[:, :rows],
            own_modes[:, rows:],
        ],
        0,
    )
    pieces = gathered(piece)
    inverse, near, weights = coarse_inverse(sub.astype(jnp.int32)[None], first, subs, mode_count)
    search_traces, modes_traces, sent = order_search(pieces, place, basis, weights, subs, rows)
    second = to_all(sent, SUB)

    image, own_search, own_res, turned = apply_flexibility(
        flex, search_traces, modes_traces, weights, own_traces, own_modes, field, own_basis, flex_modes
    )
    second = second.reshape(subs * 2 * PAD, 128)
    low, high, direction, sums = project_direction(
        second, near, turned, image, own_search, own_res, subs
    )
    totals = from_all(sums, ALL)
    totals = totals.sum(0)

    after = moved_along(low, -1)
    share = loads // lanes
    weights = last_weights(place, second, inverse, near, subs, mode_count, share)
    weights = weights + core_swap(weights)
    return results(totals, direction, own_res, high, after, turned, live, along_x(weights))


def solution(mesh):
    finer = Mesh(mesh.devices.reshape(8, 4, 4, 2), ALL)
    return jax.shard_map(
        per_device,
        mesh=finer,
        in_specs=(
            P(SUB, IFC, None),
            P(SUB, None, IFC, None),
            P(SUB, None, IFC, None),
            P(SUB, None, None, IFC),
            P(SUB),
        ),
        out_specs=(P(SUB, IFC, None), P(SUB, IFC, None)),
        check_vma=False,
    )
```

```python
import jax
import jax.numpy as jnp
from jax import lax
from jax.experimental import pallas as pl
from jax.experimental.pallas import tpu as pltpu
from jax.sharding import Mesh
from jax.sharding import PartitionSpec as P


SUB = ("z", "y")
IFC = ("x", "c")
ALL = SUB + IFC
HIGH = lax.Precision.HIGHEST
NEAR = 5
PAD = 8


def dot(a, b):
    return jnp.dot(a, b, precision=HIGH, preferred_element_type=jnp.float32)


def dot_nt(a, b):
    return lax.dot_general(
        a, b, (((1,), (1,)), ((), ())), precision=HIGH, preferred_element_type=jnp.float32
    )


def inverse_kernel(subs, modes, sub_ref, sent_ref, inverse_ref, near_ref, weights_ref, cols_ref):
    lanes = 128
    for i in range(PAD):
        rows = sent_ref[pl.ds(PAD + i, subs, stride=2 * PAD), :]
        turned = jnp.concatenate([rows] * (lanes // subs), axis=0).T
        cols_ref[pl.ds(i, 3 * PAD, stride=PAD), :] = turned[: 3 * PAD]

    def column(b, j):
        start = (b * PAD + j) * PAD
        return cols_ref[start : start + PAD, :]

    sublane = lax.broadcasted_iota(jnp.int32, (PAD, lanes), 0)
    lane = lax.broadcasted_iota(jnp.int32, (PAD, lanes), 1)
    lane_mode = lane // subs
    row_sub = lax.broadcasted_iota(jnp.int32, (subs, lanes), 0)
    lane_sub = lax.broadcasted_iota(jnp.int32, (subs, lanes), 1) % subs

    def inverse(a):
        a = list(a)
        for k in range(modes):
            pivot = 1.0 / a[k][k : k + 1, :]
            is_k = sublane == k
            for j in range(modes):
                if j != k:
                    scaled = a[j][k : k + 1, :] * pivot
                    a[j] = jnp.where(is_k, scaled, a[j] - a[k] * scaled)
            a[k] = jnp.where(is_k, pivot, -a[k] * pivot)
        return a

    def product(a, b):
        out = []
        for j in range(modes):
            total = a[0] * b[j][0:1, :]
            for k in range(1, modes):
                total = total + a[k] * b[j][k : k + 1, :]
            out.append(total)
        return out

    def moved(a, shift):
        return [pltpu.roll(x, shift % lanes, 1) for x in a]

    def dense(parts):
        halves = []
        for half in range(2):
            rows_of = []
            for a, shift in parts:
                chosen = jnp.zeros((PAD, lanes), jnp.float32)
                for q in range(lanes // subs):
                    k = half * (lanes // subs) + q
                    if k < modes:
                        chosen = jnp.where(lane_mode == q, a[k], chosen)
                rows_of.append((chosen, row_sub == lane_sub + shift))
            strips = []
            for i in range(PAD):
                strip = jnp.zeros((subs, lanes), jnp.float32)
                for chosen, mask in rows_of:
                    strip = jnp.where(mask, chosen[i : i + 1, :], strip)
                strips.append(strip)
            halves.append(jnp.concatenate(strips, axis=0))
        return jnp.concatenate(halves, axis=1)

    lower = [column(0, j) for j in range(modes)]
    diag = [column(1, j) for j in range(modes)]
    upper = [column(2, j) for j in range(modes)]
    ident = [jnp.where(sublane == k, 1.0, 0.0) for k in range(modes)]
    total = None
    h = 1
    while h < subs:
        inv = inverse(diag)
        alpha = product(lower, moved(inv, h))
        gamma = product(upper, moved(inv, -h))
        upper_before, lower_before = moved(upper, h), moved(lower, h)
        upper_after, lower_after = moved(upper, -h), moved(lower, -h)
        first = product(alpha, upper_before)
        second = product(gamma, lower_after)
        diag = [d - f - g for d, f, g in zip(diag, first, second)]
        lower = [-x for x in product(alpha, lower_before)]
        upper = [-x for x in product(gamma, upper_after)]
        step = dense(
            [
                (ident, 0),
                ([-x for x in moved(alpha, -h)], h),
                ([-x for x in moved(gamma, h)], -h),
            ]
        )
        total = step if total is None else dot(step, total)
        h *= 2
    whole = dot(dense([(inverse(diag), 0)]), total)
    inverse_ref[...] = whole
    row = lax.broadcasted_iota(jnp.int32, (NEAR * PAD, PAD * subs), 0)
    col = lax.broadcasted_iota(jnp.int32, (NEAR * PAD, PAD * subs), 1)
    wanted = (row % PAD) * subs + row // PAD + (sub_ref[0] - NEAR // 2)
    inside = (row // PAD + sub_ref[0] >= NEAR // 2) & (row // PAD + sub_ref[0] < subs + NEAR // 2)
    near = dot(jnp.where((col == wanted) & inside, 1.0, 0.0), whole)
    near_ref[...] = near
    rhs = jnp.concatenate(
        [sent_ref[pl.ds(i, subs, stride=2 * PAD), :] for i in range(PAD)], axis=0
    )
    weights_ref[...] = dot(near, rhs)


def coarse_inverse(sub, sent, subs, modes):
    size = subs * PAD
    vmem = pl.BlockSpec(memory_space=pltpu.VMEM)
    return pl.pallas_call(
        lambda *refs: inverse_kernel(subs, modes, *refs),
        out_shape=[
            jax.ShapeDtypeStruct((size, size), jnp.float32),
            jax.ShapeDtypeStruct((NEAR * PAD, size), jnp.float32),
            jax.ShapeDtypeStruct((NEAR * PAD, 128), jnp.float32),
        ],
        in_specs=[pl.BlockSpec(memory_space=pltpu.SMEM), vmem],
        out_specs=[vmem] * 3,
        scratch_shapes=[pltpu.VMEM((3 * PAD * PAD, 128), jnp.float32)],
        name="coarse_inverse",
    )(sub, sent)


def each_piece(pieces, place_ref, copy):
    count = len(pieces) // 2
    for d in range(count):
        q = lax.rem(place_ref[0] - d + count, count)
        copy(pieces[d], 2 * q + place_ref[1])
        copy(pieces[count + d], 2 * q + 1 - place_ref[1])


def dot3(a, b):
    a_high, b_high = a.astype(jnp.bfloat16), b.astype(jnp.bfloat16)
    a_low = (a - a_high.astype(jnp.float32)).astype(jnp.bfloat16)
    b_low = (b - b_high.astype(jnp.float32)).astype(jnp.bfloat16)

    def part(x, y):
        return jnp.dot(x, y, preferred_element_type=jnp.float32)

    return part(a_high, b_high) + (part(a_high, b_low) + part(a_low, b_high))


def turned_into(ext_ref, rows_ref, count):
    filler = jnp.zeros((128 - rows_ref.shape[0], 128), jnp.float32)
    for at in range(count):
        lanes = slice(at * 128, (at + 1) * 128)
        ext_ref[lanes, 128:] = jnp.concatenate([rows_ref[:, lanes], filler], 0).T


VMEM = pl.BlockSpec(memory_space=pltpu.VMEM)
SMEM = pl.BlockSpec(memory_space=pltpu.SMEM)


def shapes(*dims):
    return [jax.ShapeDtypeStruct(d, jnp.float32) for d in dims]


def stiff_kernel(rows, count, *refs):
    pieces, refs = refs[: 2 * count], refs[2 * count :]
    place_ref, rest_ref, stiff_ref, up_ref, down_ref, image_ref, basis_ref, sent_ref, ext_ref = refs
    face = 2 * count * rows
    basis_ref[2 * PAD :, :face] = jnp.zeros((PAD, face), jnp.float32)
    basis_ref[:PAD, face:] = jnp.zeros((PAD, face), jnp.float32)

    def copy(ref, at):
        for side in range(2):
            start = pl.multiple_of(side * face + at * rows, rows)
            ext_ref[pl.ds(start, rows), :128] = ref[side * rows : (side + 1) * rows, :]
        lanes = pl.ds(pl.multiple_of(at * rows, rows), rows)
        basis_ref[: 2 * PAD, lanes] = ref[2 * rows : 2 * rows + 2 * PAD, :]
        lanes = pl.ds(pl.multiple_of(face + at * rows, rows), rows)
        basis_ref[PAD:, lanes] = ref[2 * rows + 2 * PAD :, :]

    each_piece(pieces, place_ref, copy)
    turned_into(ext_ref, basis_ref, 2 * face // 128)
    ext = ext_ref[...]
    image = 0.25 * dot3(stiff_ref[...], ext)
    modes_image = image[:, 128:].T[: 3 * PAD]
    up_ref[:rows] = image[rows:, :128]
    up_ref[rows:] = modes_image[:, rows:]
    down_ref[:rows] = image[:rows, :128]
    down_ref[rows:] = modes_image[:, :rows]
    image_ref[...] = modes_image
    coarse = dot(basis_ref[PAD : 2 * PAD, :], ext)
    coarse = jnp.concatenate([coarse[:, :128], coarse[:, 128:] + rest_ref[...]], 0)
    for t in range(sent_ref.shape[0]):
        sent_ref[t] = coarse


def apply_stiffness(pieces, place, rest, stiff, subs):
    rows, face = stiff.shape[0] // 2, stiff.shape[1] // 2
    return pl.pallas_call(
        lambda *refs: stiff_kernel(rows, len(pieces) // 2, *refs),
        out_shape=shapes(
            (rows + 3 * PAD, 128), (rows + 3 * PAD, 128), (3 * PAD, 2 * rows), (3 * PAD, 2 * face),
            (subs, 2 * PAD, 128),
        ),
        in_specs=[VMEM] * len(pieces) + [SMEM, VMEM, VMEM],
        out_specs=[VMEM] * 5,
        scratch_shapes=[pltpu.VMEM((2 * face, 256), jnp.float32)],
        name="apply_stiffness",
    )(*pieces, place, rest, stiff)


def search_kernel(share, *refs):
    pieces, (place_ref, weights_ref, sent_ref) = refs[:-3], refs[-3:]
    wide = NEAR * PAD
    sums = pieces[0][...]
    for ref in pieces[1:]:
        sums = sums + ref[...]
    weights = jnp.concatenate([weights_ref[...], jnp.zeros((128 - wide, 128), jnp.float32)], 0)
    rows = sums[: 4 * PAD] - dot(sums[4 * PAD :], weights)
    lane = lax.broadcasted_iota(jnp.int32, (PAD, 128), 1)
    mine = (place_ref[0] * 2 + place_ref[1]) * share
    tail = jnp.zeros((PAD, 128), jnp.float32)
    for b in range(3):
        block = rows[b * PAD : (b + 1) * PAD]
        block = pltpu.roll(block, lax.rem(128 - mine + b * share, 128), 1)
        tail = jnp.where(lane // share == b, block, tail)
    for b in range(3):
        low = 3 * share + b * 3 * PAD
        block = pltpu.roll(sums[(4 + b) * PAD : (5 + b) * PAD], (low - wide) % 128, 1)
        tail = jnp.where((lane >= low) & (lane < low + 3 * PAD), block, tail)
    sent = jnp.concatenate([rows[3 * PAD :], tail], 0)
    for t in range(sent_ref.shape[0]):
        sent_ref[t] = sent


def search_rows(pieces, place, weights, subs):
    return pl.pallas_call(
        lambda *refs: search_kernel(128 // len(pieces), *refs),
        grid=(1,),
        out_shape=shapes((subs, 2 * PAD, 128))[0],
        in_specs=[pl.BlockSpec((8 * PAD, 128), lambda i: (0, 0))] * len(pieces)
        + [SMEM, pl.BlockSpec(weights.shape, lambda i: (0, 0))],
        out_specs=pl.BlockSpec((subs, 2 * PAD, 128), lambda i: (0, 0, 0)),
        name="search_rows",
    )(*pieces, place, weights)


def flex_kernel(rows, count, *refs):
    pieces, refs = refs[: 2 * count], refs[2 * count :]
    place_ref, flex_ref, weights_ref, own_ref, own_modes_ref, field_ref, own_basis_ref, flex_modes_ref = refs[:8]
    image_ref, search_ref, res_ref, turned_ref, ext_ref = refs[8:]
    face = 2 * count * rows
    wide = NEAR * PAD
    head = 8 * PAD
    weights = jnp.concatenate([weights_ref[...], jnp.zeros((128 - wide, 128), jnp.float32)], 0)
    filler = jnp.zeros((128 - wide, rows), jnp.float32)

    def copy(ref, at):
        for side in range(2):
            at_rows = pl.ds(pl.multiple_of(side * face + at * rows, rows), rows)
            ext_ref[at_rows, :128] = ref[head + side * rows : head + (side + 1) * rows, :]
            low = head + 2 * rows + side * wide
            ext_ref[at_rows, 128:] = jnp.concatenate([ref[low : low + wide, :], filler], 0).T

    each_piece(pieces, place_ref, copy)
    both = dot3(flex_ref[...], ext_ref[...])
    image_ref[...] = both[:, :128] - dot(both[:, 128:], weights)
    own_modes = jnp.concatenate(
        [own_modes_ref[...], jnp.zeros((128 - wide, 2 * rows), jnp.float32)], 0
    ).T
    search_ref[...] = own_ref[...] - dot(own_modes, weights)
    turned = jnp.concatenate(
        [
            flex_modes_ref[...], own_basis_ref[...],
            jnp.zeros((128 - 6 * PAD, 2 * rows), jnp.float32),
        ],
        0,
    ).T
    turned_ref[...] = turned
    gap = jnp.zeros((3 * PAD, 128), jnp.float32)
    none = jnp.zeros((128 - 6 * PAD, 128), jnp.float32)
    shifted = jnp.concatenate([gap, weights_ref[PAD : 4 * PAD, :], none], 0)
    res_ref[...] = field_ref[...] - dot(turned[rows:], shifted)


def apply_flexibility(pieces, place, flex, weights, own, own_modes, field, own_basis, flex_modes):
    rows = field.shape[0]
    return pl.pallas_call(
        lambda *refs: flex_kernel(rows, len(pieces) // 2, *refs),
        out_shape=shapes((2 * rows, 128), (2 * rows, 128), (rows, 128), (2 * rows, 128)),
        in_specs=[VMEM] * len(pieces) + [SMEM] + [VMEM] * 7,
        out_specs=[VMEM] * 4,
        scratch_shapes=[pltpu.VMEM((2 * len(pieces) * rows, 256), jnp.float32)],
        name="apply_flexibility",
    )(*pieces, place, flex, weights, own, own_modes, field, own_basis, flex_modes)


def chosen(a, choice):
    total = None
    for _ in range(3):
        part = a.astype(jnp.bfloat16)
        a = a - part.astype(jnp.float32)
        term = jnp.dot(part, choice, preferred_element_type=jnp.float32)
        total = term if total is None else total + term
    return total


def last_kernel(subs, modes, share, place_ref, second_ref, inverse_ref, near_ref, out_ref):
    mine = (place_ref[0] * 2 + place_ref[1]) * share
    lane = lax.broadcasted_iota(jnp.int32, (subs, 128), 1)
    row = lax.broadcasted_iota(jnp.int32, (subs, 128), 0)
    rhs = jnp.concatenate(
        [second_ref[pl.ds(i, subs, stride=2 * PAD), :] for i in range(PAD)], axis=0
    )
    weights = dot(inverse_ref[...], pltpu.roll(rhs, lax.rem(128 - mine, 128), 1))

    def earlier(x):
        return jnp.where(row == 0, 0.0, pltpu.roll(x, 1, 0))

    def later(x):
        return jnp.where(row == subs - 1, 0.0, pltpu.roll(x, subs - 1, 0))

    here = jnp.zeros((subs, 128), jnp.float32)
    for k in range(modes):
        block = weights[k * subs : (k + 1) * subs]
        here = jnp.where(lane // share == k, pltpu.roll(block, k * share, 1), here)
    near = (earlier(here), here, later(here))
    tails = jnp.concatenate(
        [second_ref[pl.ds(PAD + i, subs, stride=2 * PAD), :] for i in range(PAD)], axis=0
    )
    source = lax.broadcasted_iota(jnp.int32, (128, 9 * 128), 0)
    target = lax.broadcasted_iota(jnp.int32, (128, 9 * 128), 1)
    wanted = 3 * share + (target // 128) * PAD + (target % 128) // share
    factors = chosen(tails, (source == wanted).astype(jnp.float32).astype(jnp.bfloat16))
    products = []
    for b in range(3):
        strips = []
        for i in range(PAD):
            strip = jnp.zeros((subs, 128), jnp.float32)
            for c in range(3):
                at = (b * 3 + c) * 128
                strip = strip + factors[i * subs : (i + 1) * subs, at : at + 128] * near[c]
            strips.append(strip)
        products.append(jnp.concatenate(strips, 0))
    source = lax.broadcasted_iota(jnp.int32, (128, 128), 0)
    target = lax.broadcasted_iota(jnp.int32, (128, 128), 1)
    added = chosen(
        jnp.concatenate(products, 0),
        ((source % share == target) & (source < modes * share)).astype(jnp.float32).astype(jnp.bfloat16),
    )
    out = []
    for i in range(PAD):
        parts = []
        for b in range(3):
            tail = tails[i * subs : (i + 1) * subs]
            tail = tail if b == 0 else pltpu.roll(tail, 128 - b * share, 1)
            start = (b * PAD + i) * subs
            parts.append(tail - added[start : start + subs])
        total = parts[1] + later(parts[0]) + earlier(parts[2])
        out.append(jnp.where(lane < share, total, 0.0))
    last = dot(near_ref[PAD : 4 * PAD, :], jnp.concatenate(out, 0))
    out_ref[...] = pltpu.roll(last, mine, 1)


def last_weights(place, second, inverse, near, subs, modes, share):
    return pl.pallas_call(
        lambda *refs: last_kernel(subs, modes, share, *refs),
        out_shape=shapes((3 * PAD, 128))[0],
        in_specs=[SMEM] + [VMEM] * 3,
        out_specs=VMEM,
        name="last_weights",
    )(place, second, inverse, near)


def direction_kernel(subs, second_ref, near_ref, turned_ref, image_ref, search_ref, res_ref, low_ref, high_ref,
                     direction_ref, sums_ref):
    rows = res_ref.shape[0]
    rhs = jnp.concatenate(
        [second_ref[pl.ds(i, subs, stride=2 * PAD), :] for i in range(PAD)], axis=0
    )
    weights = dot(near_ref[PAD : 4 * PAD, :], rhs)
    none = jnp.zeros((128 - 6 * PAD, 128), jnp.float32)
    gap = jnp.zeros((3 * PAD, 128), jnp.float32)
    both = jnp.concatenate(
        [
            jnp.concatenate([weights, gap, none], 0),
            jnp.concatenate([gap, weights, none], 0),
        ],
        1,
    )
    change = dot(turned_ref[...], both)
    image = image_ref[...] - change[:, :128]
    direction = search_ref[...] - change[:, 128:]
    low_ref[...] = image[:rows]
    high_ref[...] = image[rows:]
    direction_ref[...] = direction[rows:]
    first = jnp.sum(res_ref[...] * search_ref[rows:, :], axis=0, keepdims=True)
    second = jnp.sum(direction * image, axis=0, keepdims=True)
    sums_ref[...] = jnp.broadcast_to(jnp.concatenate([first, second], 0)[None], sums_ref.shape)


def project_direction(second, near, turned, image, search, res, subs, devices):
    rows = res.shape[0]
    return pl.pallas_call(
        lambda *refs: direction_kernel(subs, *refs),
        out_shape=shapes((rows, 128), (rows, 128), (rows, 128), (devices, 2, 128)),
        in_specs=[VMEM] * 6,
        out_specs=[VMEM] * 4,
        name="project_direction",
    )(second, near, turned, image, search, res)


def result_kernel(totals_ref, direction_ref, res_ref, high_ref, after_ref, turned_ref, live_ref, *refs):
    parts, (multipliers_ref, residual_ref) = refs[:-2], refs[-2:]
    weights = parts[0][...]
    for part in parts[1:]:
        weights = weights + part[...]
    rows = res_ref.shape[0]
    gap = jnp.zeros((3 * PAD, 128), jnp.float32)
    none = jnp.zeros((128 - 6 * PAD, 128), jnp.float32)
    change = dot(turned_ref[rows:, :], jnp.concatenate([gap, weights, none], 0))
    step = totals_ref[0:1, :] / totals_ref[1:2, :]
    image = (high_ref[...] - after_ref[...]) * live_ref[0] - change
    multipliers_ref[0] = step * direction_ref[...]
    residual_ref[0] = res_ref[...] - step * image


def results(totals, direction, res, high, after, turned, live, parts):
    return pl.pallas_call(
        result_kernel,
        out_shape=shapes((1, *res.shape), (1, *res.shape)),
        in_specs=[VMEM] * 6 + [SMEM] + [VMEM] * len(parts),
        out_specs=[VMEM] * 2,
        name="results",
    )(totals, direction, res, high, after, turned, live[None], *parts)


def moved_along(block, distance):
    n = lax.axis_size(SUB)
    return lax.ppermute(
        block, SUB, [(i - distance, i) for i in range(n) if 0 <= i - distance < n]
    )


def core_swap(block):
    return lax.ppermute(block, "c", [(0, 1), (1, 0)])


def along_x(piece):
    n = lax.axis_size("x")
    return [piece] + [
        lax.ppermute(piece, "x", [(i, (i + d) % n) for i in range(n)]) for d in range(1, n)
    ]


def to_all(values, axis):
    return lax.all_to_all(values, axis, 0, 0, tiled=True)


def gathered(piece):
    pieces = along_x(piece)
    return pieces + [core_swap(part) for part in pieces]


def per_device(gap, flexibility, stiffness, modes, mode_counts):
    subs = lax.axis_size(SUB)
    sub = lax.axis_index(SUB)
    place = jnp.stack([lax.axis_index("x"), lax.axis_index("c")]).astype(jnp.int32)
    rows, loads = gap.shape[1], gap.shape[2]
    lanes = lax.axis_size(IFC)
    face = rows * lanes
    mode_count = modes.shape[1]
    live = (sub < subs - 1).astype(jnp.float32)
    inner = (sub > 0).astype(jnp.float32)
    flex = flexibility.reshape(2 * rows, 2 * face)
    stiff = stiffness.reshape(2 * rows, 2 * face)

    active = (jnp.arange(PAD) < jnp.minimum(mode_counts[0], mode_count)).astype(jnp.float32)
    padded = jnp.pad(modes[0], ((0, PAD - mode_count), (0, 0), (0, 0))) * active[:, None, None]
    left, right = padded[:, 0], padded[:, 1] * live
    field = gap[0] * live

    from_before = moved_along(jnp.concatenate([field, right], 0), 1)
    left_after = moved_along(left, -1)
    field_before, right_before = from_before[:rows], from_before[rows:]
    left_in = left * inner
    piece = jnp.concatenate([-field_before, field, -right_before, left_in, right, -left_after], 0)
    none = jnp.zeros_like(left)
    own_basis = jnp.concatenate(
        [
            jnp.concatenate([-right_before, left_in, none], 0),
            jnp.concatenate([none, right, -left_after], 0),
        ],
        1,
    )
    rest = jnp.pad(
        jnp.eye(PAD, dtype=jnp.float32) * (1.0 - active)[:, None], ((0, 0), (PAD, 128 - 2 * PAD))
    )
    up, down, modes_image, basis, sent = apply_stiffness(gathered(piece), place, rest, stiff, subs)
    first = to_all(sent, SUB).reshape(subs * 2 * PAD, 128)
    before = moved_along(up, 1)
    after = moved_along(down, -1)
    top = (down[:rows] - before[:rows]) * inner
    bottom = (up[:rows] - after[:rows]) * live
    own_traces = jnp.concatenate([top, bottom], 0)
    gone = jnp.zeros((PAD, rows), jnp.float32)
    modes_top = jnp.concatenate([gone, modes_image[:, :rows], gone], 0)
    modes_top = modes_top - jnp.concatenate([before[rows:], gone, gone], 0)
    modes_bottom = jnp.concatenate([gone, modes_image[:, rows:], gone], 0)
    modes_bottom = modes_bottom - jnp.concatenate([gone, gone, after[rows:]], 0)
    own_modes = jnp.concatenate([modes_top * inner, modes_bottom * live], 1)

    flex_modes = dot_nt(basis, flex)
    tests = jnp.concatenate([flex_modes, own_basis[PAD : 2 * PAD]], 0)
    small = dot_nt(tests, jnp.concatenate([own_modes, own_basis], 0))
    piece = jnp.concatenate(
        [
            dot(tests, own_traces), jnp.pad(small, ((0, 0), (0, 128 - small.shape[1]))), own_traces,
            own_modes[:, :rows], own_modes[:, rows:],
        ],
        0,
    )
    pieces = gathered(piece)
    inverse, near, weights = coarse_inverse(sub.astype(jnp.int32)[None], first, subs, mode_count)
    sent = search_rows(pieces, place, weights, subs)
    second = to_all(sent, SUB)

    image, own_search, own_res, turned = apply_flexibility(
        pieces, place, flex, weights, own_traces, own_modes, field, own_basis, flex_modes
    )
    second = second.reshape(subs * 2 * PAD, 128)
    low, high, direction, sums = project_direction(
        second, near, turned, image, own_search, own_res, subs, lax.axis_size(ALL)
    )
    totals = to_all(sums, ALL)
    totals = totals.sum(0)

    after = moved_along(low, -1)
    share = loads // lanes
    weights = last_weights(place, second, inverse, near, subs, mode_count, share)
    swapped = core_swap(weights)
    weights = weights + swapped
    return results(totals, direction, own_res, high, after, turned, live, along_x(weights))


def solution(mesh):
    finer = Mesh(mesh.devices.reshape(8, 4, 4, 2), ALL)
    return jax.shard_map(
        per_device,
        mesh=finer,
        in_specs=(
            P(SUB, IFC, None),
            P(SUB, None, IFC, None),
            P(SUB, None, IFC, None),
            P(SUB, None, None, IFC),
            P(SUB),
        ),
        out_specs=(P(SUB, IFC, None), P(SUB, IFC, None)),
        check_vma=False,
    )
```

```python
import jax
import jax.numpy as jnp
from jax import lax
from jax.experimental import pallas as pl
from jax.experimental.pallas import tpu as pltpu
from jax.sharding import Mesh
from jax.sharding import PartitionSpec as P


SUB = ("z", "y")
IFC = ("x", "c")
ALL = SUB + IFC
HIGH = lax.Precision.HIGHEST
NEAR = 5
PAD = 8


def dot(a, b):
    return jnp.dot(a, b, precision=HIGH, preferred_element_type=jnp.float32)


def dot_nt(a, b):
    return lax.dot_general(
        a, b, (((1,), (1,)), ((), ())), precision=HIGH, preferred_element_type=jnp.float32
    )


def inverse_kernel(subs, modes, sub_ref, sent_ref, inverse_ref, near_ref, weights_ref, cols_ref):
    lanes = 128
    for i in range(PAD):
        rows = sent_ref[pl.ds(PAD + i, subs, stride=2 * PAD), :]
        turned = jnp.concatenate([rows] * (lanes // subs), axis=0).T
        cols_ref[pl.ds(i, 3 * PAD, stride=PAD), :] = turned[: 3 * PAD]

    def column(b, j):
        start = (b * PAD + j) * PAD
        return cols_ref[start : start + PAD, :]

    sublane = lax.broadcasted_iota(jnp.int32, (PAD, lanes), 0)
    lane = lax.broadcasted_iota(jnp.int32, (PAD, lanes), 1)
    lane_mode = lane // subs
    row_sub = lax.broadcasted_iota(jnp.int32, (subs, lanes), 0)
    lane_sub = lax.broadcasted_iota(jnp.int32, (subs, lanes), 1) % subs

    def inverse(a):
        a = list(a)
        for k in range(modes):
            pivot = 1.0 / a[k][k : k + 1, :]
            is_k = sublane == k
            for j in range(modes):
                if j != k:
                    scaled = a[j][k : k + 1, :] * pivot
                    a[j] = jnp.where(is_k, scaled, a[j] - a[k] * scaled)
            a[k] = jnp.where(is_k, pivot, -a[k] * pivot)
        return a

    def product(a, b):
        out = []
        for j in range(modes):
            total = a[0] * b[j][0:1, :]
            for k in range(1, modes):
                total = total + a[k] * b[j][k : k + 1, :]
            out.append(total)
        return out

    def moved(a, shift):
        return [pltpu.roll(x, shift % lanes, 1) for x in a]

    def dense(parts):
        halves = []
        for half in range(2):
            rows_of = []
            for a, shift in parts:
                chosen = jnp.zeros((PAD, lanes), jnp.float32)
                for q in range(lanes // subs):
                    k = half * (lanes // subs) + q
                    if k < modes:
                        chosen = jnp.where(lane_mode == q, a[k], chosen)
                rows_of.append((chosen, row_sub == lane_sub + shift))
            strips = []
            for i in range(PAD):
                strip = jnp.zeros((subs, lanes), jnp.float32)
                for chosen, mask in rows_of:
                    strip = jnp.where(mask, chosen[i : i + 1, :], strip)
                strips.append(strip)
            halves.append(jnp.concatenate(strips, axis=0))
        return jnp.concatenate(halves, axis=1)

    lower = [column(0, j) for j in range(modes)]
    diag = [column(1, j) for j in range(modes)]
    upper = [column(2, j) for j in range(modes)]
    ident = [jnp.where(sublane == k, 1.0, 0.0) for k in range(modes)]
    total = None
    h = 1
    while h < subs:
        inv = inverse(diag)
        alpha = product(lower, moved(inv, h))
        gamma = product(upper, moved(inv, -h))
        upper_before, lower_before = moved(upper, h), moved(lower, h)
        upper_after, lower_after = moved(upper, -h), moved(lower, -h)
        first = product(alpha, upper_before)
        second = product(gamma, lower_after)
        diag = [d - f - g for d, f, g in zip(diag, first, second)]
        lower = [-x for x in product(alpha, lower_before)]
        upper = [-x for x in product(gamma, upper_after)]
        step = dense(
            [
                (ident, 0),
                ([-x for x in moved(alpha, -h)], h),
                ([-x for x in moved(gamma, h)], -h),
            ]
        )
        total = step if total is None else dot(step, total)
        h *= 2
    whole = dot(dense([(inverse(diag), 0)]), total)
    inverse_ref[...] = whole
    row = lax.broadcasted_iota(jnp.int32, (NEAR * PAD, PAD * subs), 0)
    col = lax.broadcasted_iota(jnp.int32, (NEAR * PAD, PAD * subs), 1)
    wanted = (row % PAD) * subs + row // PAD + (sub_ref[0] - NEAR // 2)
    inside = (row // PAD + sub_ref[0] >= NEAR // 2) & (row // PAD + sub_ref[0] < subs + NEAR // 2)
    near = dot(jnp.where((col == wanted) & inside, 1.0, 0.0), whole)
    near_ref[...] = near
    rhs = jnp.concatenate(
        [sent_ref[pl.ds(i, subs, stride=2 * PAD), :] for i in range(PAD)], axis=0
    )
    weights_ref[...] = dot(near, rhs)


def coarse_inverse(sub, sent, subs, modes):
    size = subs * PAD
    return local_call(
        lambda *refs: inverse_kernel(subs, modes, *refs),
        [(size, size), (NEAR * PAD, size), (NEAR * PAD, 128)], 3, [sent], [sub],
        [(3 * PAD * PAD, 128)],
    )


def each_piece(pieces, place_ref, copy):
    count = len(pieces) // 2
    for d in range(count):
        q = lax.rem(place_ref[0] - d + count, count)
        copy(pieces[d], 2 * q + place_ref[1])
        copy(pieces[count + d], 2 * q + 1 - place_ref[1])


def dot3(a, b):
    a_high, b_high = a.astype(jnp.bfloat16), b.astype(jnp.bfloat16)
    a_low = (a - a_high.astype(jnp.float32)).astype(jnp.bfloat16)
    b_low = (b - b_high.astype(jnp.float32)).astype(jnp.bfloat16)

    def part(x, y):
        return jnp.dot(x, y, preferred_element_type=jnp.float32)

    return part(a_high, b_high) + (part(a_high, b_low) + part(a_low, b_high))


def turned_into(ext_ref, rows_ref, count):
    filler = jnp.zeros((128 - rows_ref.shape[0], 128), jnp.float32)
    for at in range(count):
        lanes = slice(at * 128, (at + 1) * 128)
        ext_ref[lanes, 128:] = jnp.concatenate([rows_ref[:, lanes], filler], 0).T


VMEM = pl.BlockSpec(memory_space=pltpu.VMEM)
SMEM = pl.BlockSpec(memory_space=pltpu.SMEM)


KERNEL_BYTES = 24 << 20


def local_call(kernel, outs, kept, arrays, scalars=(), scratch=(), large=None):
    return pl.pallas_call(
        kernel,
        out_shape=[
            pltpu.VMEM(d, jnp.float32) if k < kept else jax.ShapeDtypeStruct(d, jnp.float32)
            for k, d in enumerate(outs)
        ],
        in_specs=[SMEM] * len(scalars) + [VMEM] * len(arrays),
        out_specs=[VMEM] * len(outs),
        scratch_shapes=[pltpu.VMEM(d, jnp.float32) for d in scratch],
        compiler_params=pltpu.CompilerParams(vmem_limit_bytes=KERNEL_BYTES),
    )(*scalars, *[
        a if k == large else pltpu.with_memory_space_constraint(a, pltpu.VMEM)
        for k, a in enumerate(arrays)
    ])


def stiff_kernel(rows, count, place_ref, *refs):
    pieces, refs = refs[: 2 * count], refs[2 * count :]
    rest_ref, stiff_ref, up_ref, down_ref, image_ref, basis_ref, sent_ref, ext_ref = refs
    face = 2 * count * rows
    basis_ref[2 * PAD :, :face] = jnp.zeros((PAD, face), jnp.float32)
    basis_ref[:PAD, face:] = jnp.zeros((PAD, face), jnp.float32)

    def copy(ref, at):
        for side in range(2):
            start = pl.multiple_of(side * face + at * rows, rows)
            ext_ref[pl.ds(start, rows), :128] = ref[side * rows : (side + 1) * rows, :]
        lanes = pl.ds(pl.multiple_of(at * rows, rows), rows)
        basis_ref[: 2 * PAD, lanes] = ref[2 * rows : 2 * rows + 2 * PAD, :]
        lanes = pl.ds(pl.multiple_of(face + at * rows, rows), rows)
        basis_ref[PAD:, lanes] = ref[2 * rows + 2 * PAD :, :]

    each_piece(pieces, place_ref, copy)
    turned_into(ext_ref, basis_ref, 2 * face // 128)
    ext = ext_ref[...]
    image = 0.25 * dot3(stiff_ref[...], ext)
    modes_image = image[:, 128:].T[: 3 * PAD]
    up_ref[:rows] = image[rows:, :128]
    up_ref[rows:] = modes_image[:, rows:]
    down_ref[:rows] = image[:rows, :128]
    down_ref[rows:] = modes_image[:, :rows]
    image_ref[...] = modes_image
    coarse = dot(basis_ref[PAD : 2 * PAD, :], ext)
    coarse = jnp.concatenate([coarse[:, :128], coarse[:, 128:] + rest_ref[...]], 0)
    for t in range(sent_ref.shape[0]):
        sent_ref[t] = coarse


def apply_stiffness(pieces, place, rest, stiff, subs):
    rows, face = stiff.shape[0] // 2, stiff.shape[1] // 2
    return local_call(
        lambda *refs: stiff_kernel(rows, len(pieces) // 2, *refs),
        [
            (rows + 3 * PAD, 128), (rows + 3 * PAD, 128), (3 * PAD, 2 * rows), (3 * PAD, 2 * face),
            (subs, 2 * PAD, 128),
        ],
        4, [*pieces, rest, stiff], [place], [(2 * face, 256)],
    )


def search_kernel(share, place_ref, *refs):
    pieces, (weights_ref, sent_ref) = refs[:-2], refs[-2:]
    wide = NEAR * PAD
    sums = pieces[0][: 8 * PAD, :]
    for ref in pieces[1:]:
        sums = sums + ref[: 8 * PAD, :]
    weights = jnp.concatenate([weights_ref[...], jnp.zeros((128 - wide, 128), jnp.float32)], 0)
    rows = sums[: 4 * PAD] - dot(sums[4 * PAD :], weights)
    lane = lax.broadcasted_iota(jnp.int32, (PAD, 128), 1)
    mine = (place_ref[0] * 2 + place_ref[1]) * share
    tail = jnp.zeros((PAD, 128), jnp.float32)
    for b in range(3):
        block = rows[b * PAD : (b + 1) * PAD]
        block = pltpu.roll(block, lax.rem(128 - mine + b * share, 128), 1)
        tail = jnp.where(lane // share == b, block, tail)
    for b in range(3):
        low = 3 * share + b * 3 * PAD
        block = pltpu.roll(sums[(4 + b) * PAD : (5 + b) * PAD], (low - wide) % 128, 1)
        tail = jnp.where((lane >= low) & (lane < low + 3 * PAD), block, tail)
    sent = jnp.concatenate([rows[3 * PAD :], tail], 0)
    for t in range(sent_ref.shape[0]):
        sent_ref[t] = sent


def search_rows(pieces, place, weights, subs):
    return local_call(
        lambda *refs: search_kernel(128 // len(pieces), *refs),
        [(subs, 2 * PAD, 128)], 0, [*pieces, weights], [place],
    )[0]


def flex_kernel(rows, count, place_ref, *refs):
    pieces, refs = refs[: 2 * count], refs[2 * count :]
    flex_ref, weights_ref, own_ref, own_modes_ref, field_ref, own_basis_ref, flex_modes_ref = refs[:7]
    image_ref, search_ref, res_ref, turned_ref, ext_ref = refs[7:]
    face = 2 * count * rows
    wide = NEAR * PAD
    head = 8 * PAD
    weights = jnp.concatenate([weights_ref[...], jnp.zeros((128 - wide, 128), jnp.float32)], 0)
    filler = jnp.zeros((128 - wide, rows), jnp.float32)

    def copy(ref, at):
        for side in range(2):
            at_rows = pl.ds(pl.multiple_of(side * face + at * rows, rows), rows)
            ext_ref[at_rows, :128] = ref[head + side * rows : head + (side + 1) * rows, :]
            low = head + 2 * rows + side * wide
            ext_ref[at_rows, 128:] = jnp.concatenate([ref[low : low + wide, :], filler], 0).T

    each_piece(pieces, place_ref, copy)
    both = dot3(flex_ref[...], ext_ref[...])
    image_ref[...] = both[:, :128] - dot(both[:, 128:], weights)
    own_modes = jnp.concatenate(
        [own_modes_ref[...], jnp.zeros((128 - wide, 2 * rows), jnp.float32)], 0
    ).T
    search_ref[...] = own_ref[...] - dot(own_modes, weights)
    turned = jnp.concatenate(
        [
            flex_modes_ref[...], own_basis_ref[...],
            jnp.zeros((128 - 6 * PAD, 2 * rows), jnp.float32),
        ],
        0,
    ).T
    turned_ref[...] = turned
    gap = jnp.zeros((3 * PAD, 128), jnp.float32)
    none = jnp.zeros((128 - 6 * PAD, 128), jnp.float32)
    shifted = jnp.concatenate([gap, weights_ref[PAD : 4 * PAD, :], none], 0)
    res_ref[...] = field_ref[...] - dot(turned[rows:], shifted)


def apply_flexibility(pieces, place, *arrays):
    rows = arrays[0].shape[0] // 2
    return local_call(
        lambda *refs: flex_kernel(rows, len(pieces) // 2, *refs),
        [(2 * rows, 128), (2 * rows, 128), (rows, 128), (2 * rows, 128)], 4, [*pieces, *arrays],
        [place], [(2 * len(pieces) * rows, 256)], len(pieces),
    )


def chosen(a, choice):
    total = None
    for _ in range(3):
        part = a.astype(jnp.bfloat16)
        a = a - part.astype(jnp.float32)
        term = jnp.dot(part, choice, preferred_element_type=jnp.float32)
        total = term if total is None else total + term
    return total


def last_kernel(subs, modes, share, place_ref, second_ref, inverse_ref, near_ref, out_ref):
    mine = (place_ref[0] * 2 + place_ref[1]) * share
    lane = lax.broadcasted_iota(jnp.int32, (subs, 128), 1)
    row = lax.broadcasted_iota(jnp.int32, (subs, 128), 0)
    rhs = jnp.concatenate(
        [second_ref[pl.ds(i, subs, stride=2 * PAD), :] for i in range(PAD)], axis=0
    )
    weights = dot(inverse_ref[...], pltpu.roll(rhs, lax.rem(128 - mine, 128), 1))

    def earlier(x):
        return jnp.where(row == 0, 0.0, pltpu.roll(x, 1, 0))

    def later(x):
        return jnp.where(row == subs - 1, 0.0, pltpu.roll(x, subs - 1, 0))

    here = jnp.zeros((subs, 128), jnp.float32)
    for k in range(modes):
        block = weights[k * subs : (k + 1) * subs]
        here = jnp.where(lane // share == k, pltpu.roll(block, k * share, 1), here)
    near = (earlier(here), here, later(here))
    tails = jnp.concatenate(
        [second_ref[pl.ds(PAD + i, subs, stride=2 * PAD), :] for i in range(PAD)], axis=0
    )
    source = lax.broadcasted_iota(jnp.int32, (128, 9 * 128), 0)
    target = lax.broadcasted_iota(jnp.int32, (128, 9 * 128), 1)
    wanted = 3 * share + (target // 128) * PAD + (target % 128) // share
    factors = chosen(tails, (source == wanted).astype(jnp.float32).astype(jnp.bfloat16))
    products = []
    for b in range(3):
        strips = []
        for i in range(PAD):
            strip = jnp.zeros((subs, 128), jnp.float32)
            for c in range(3):
                at = (b * 3 + c) * 128
                strip = strip + factors[i * subs : (i + 1) * subs, at : at + 128] * near[c]
            strips.append(strip)
        products.append(jnp.concatenate(strips, 0))
    source = lax.broadcasted_iota(jnp.int32, (128, 128), 0)
    target = lax.broadcasted_iota(jnp.int32, (128, 128), 1)
    added = chosen(
        jnp.concatenate(products, 0),
        ((source % share == target) & (source < modes * share)).astype(jnp.float32).astype(jnp.bfloat16),
    )
    out = []
    for i in range(PAD):
        parts = []
        for b in range(3):
            tail = tails[i * subs : (i + 1) * subs]
            tail = tail if b == 0 else pltpu.roll(tail, 128 - b * share, 1)
            start = (b * PAD + i) * subs
            parts.append(tail - added[start : start + subs])
        total = parts[1] + later(parts[0]) + earlier(parts[2])
        out.append(jnp.where(lane < share, total, 0.0))
    last = dot(near_ref[PAD : 4 * PAD, :], jnp.concatenate(out, 0))
    out_ref[...] = pltpu.roll(last, mine, 1)


def last_weights(place, second, inverse, near, subs, modes, share):
    return local_call(
        lambda *refs: last_kernel(subs, modes, share, *refs),
        [(3 * PAD, 128)], 1, [second, inverse, near], [place],
    )[0]


def direction_kernel(subs, second_ref, near_ref, turned_ref, image_ref, search_ref, res_ref, low_ref, high_ref,
                     direction_ref, sums_ref):
    rows = res_ref.shape[0]
    rhs = jnp.concatenate(
        [second_ref[pl.ds(i, subs, stride=2 * PAD), :] for i in range(PAD)], axis=0
    )
    weights = dot(near_ref[PAD : 4 * PAD, :], rhs)
    none = jnp.zeros((128 - 6 * PAD, 128), jnp.float32)
    gap = jnp.zeros((3 * PAD, 128), jnp.float32)
    both = jnp.concatenate(
        [
            jnp.concatenate([weights, gap, none], 0),
            jnp.concatenate([gap, weights, none], 0),
        ],
        1,
    )
    change = dot(turned_ref[...], both)
    image = image_ref[...] - change[:, :128]
    direction = search_ref[...] - change[:, 128:]
    low_ref[...] = image[:rows]
    high_ref[...] = image[rows:]
    direction_ref[...] = direction[rows:]
    first = jnp.sum(res_ref[...] * search_ref[rows:, :], axis=0, keepdims=True)
    second = jnp.sum(direction * image, axis=0, keepdims=True)
    sums_ref[...] = jnp.broadcast_to(jnp.concatenate([first, second], 0)[None], sums_ref.shape)


def project_direction(second, near, turned, image, search, res, subs, devices):
    rows = res.shape[0]
    return local_call(
        lambda *refs: direction_kernel(subs, *refs),
        [(rows, 128), (rows, 128), (rows, 128), (devices, 2, 128)], 3,
        [second, near, turned, image, search, res],
    )


def result_kernel(live_ref, totals_ref, direction_ref, res_ref, high_ref, after_ref, turned_ref, *refs):
    parts, (multipliers_ref, residual_ref) = refs[:-2], refs[-2:]
    weights = parts[0][...]
    for part in parts[1:]:
        weights = weights + part[...]
    rows = res_ref.shape[0]
    gap = jnp.zeros((3 * PAD, 128), jnp.float32)
    none = jnp.zeros((128 - 6 * PAD, 128), jnp.float32)
    change = dot(turned_ref[rows:, :], jnp.concatenate([gap, weights, none], 0))
    step = totals_ref[0:1, :] / totals_ref[1:2, :]
    image = (high_ref[...] - after_ref[...]) * live_ref[0] - change
    multipliers_ref[0] = step * direction_ref[...]
    residual_ref[0] = res_ref[...] - step * image


def results(totals, direction, res, high, after, turned, live, parts):
    return local_call(
        result_kernel, [(1, *res.shape)] * 2, 0,
        [totals, direction, res, high, after, turned, *parts], [live[None]],
    )


def moved_along(block, distance):
    n = lax.axis_size(SUB)
    return lax.ppermute(
        block, SUB, [(i - distance, i) for i in range(n) if 0 <= i - distance < n]
    )


def core_swap(block):
    return lax.ppermute(block, "c", [(0, 1), (1, 0)])


def along_x(piece):
    n = lax.axis_size("x")
    return [piece] + [
        lax.ppermute(piece, "x", [(i, (i + d) % n) for i in range(n)]) for d in range(1, n)
    ]


def to_all(values, axis):
    return lax.all_to_all(values, axis, 0, 0, tiled=True)


def gathered(piece):
    pieces = along_x(piece)
    return pieces + [core_swap(part) for part in pieces]


def per_device(gap, flexibility, stiffness, modes, mode_counts):
    subs = lax.axis_size(SUB)
    sub = lax.axis_index(SUB)
    place = jnp.stack([lax.axis_index("x"), lax.axis_index("c")]).astype(jnp.int32)
    rows, loads = gap.shape[1], gap.shape[2]
    lanes = lax.axis_size(IFC)
    face = rows * lanes
    mode_count = modes.shape[1]
    live = (sub < subs - 1).astype(jnp.float32)
    inner = (sub > 0).astype(jnp.float32)
    flex = flexibility.reshape(2 * rows, 2 * face)
    stiff = stiffness.reshape(2 * rows, 2 * face)

    active = (jnp.arange(PAD) < jnp.minimum(mode_counts[0], mode_count)).astype(jnp.float32)
    padded = jnp.pad(modes[0], ((0, PAD - mode_count), (0, 0), (0, 0))) * active[:, None, None]
    left, right = padded[:, 0], padded[:, 1] * live
    field = gap[0] * live

    from_before = moved_along(jnp.concatenate([field, right], 0), 1)
    left_after = moved_along(left, -1)
    field_before, right_before = from_before[:rows], from_before[rows:]
    left_in = left * inner
    piece = jnp.concatenate([-field_before, field, -right_before, left_in, right, -left_after], 0)
    none = jnp.zeros_like(left)
    own_basis = jnp.concatenate(
        [
            jnp.concatenate([-right_before, left_in, none], 0),
            jnp.concatenate([none, right, -left_after], 0),
        ],
        1,
    )
    rest = jnp.pad(
        jnp.eye(PAD, dtype=jnp.float32) * (1.0 - active)[:, None], ((0, 0), (PAD, 128 - 2 * PAD))
    )
    up, down, modes_image, basis, sent = apply_stiffness(gathered(piece), place, rest, stiff, subs)
    first = to_all(sent, SUB).reshape(subs * 2 * PAD, 128)
    before = moved_along(up, 1)
    after = moved_along(down, -1)
    top = (down[:rows] - before[:rows]) * inner
    bottom = (up[:rows] - after[:rows]) * live
    own_traces = jnp.concatenate([top, bottom], 0)
    gone = jnp.zeros((PAD, rows), jnp.float32)
    modes_top = jnp.concatenate([gone, modes_image[:, :rows], gone], 0)
    modes_top = modes_top - jnp.concatenate([before[rows:], gone, gone], 0)
    modes_bottom = jnp.concatenate([gone, modes_image[:, rows:], gone], 0)
    modes_bottom = modes_bottom - jnp.concatenate([gone, gone, after[rows:]], 0)
    own_modes = jnp.concatenate([modes_top * inner, modes_bottom * live], 1)

    flex_modes = dot_nt(basis, flex)
    tests = jnp.concatenate([flex_modes, own_basis[PAD : 2 * PAD]], 0)
    small = dot_nt(tests, jnp.concatenate([own_modes, own_basis], 0))
    piece = jnp.concatenate(
        [
            dot(tests, own_traces), jnp.pad(small, ((0, 0), (0, 128 - small.shape[1]))), own_traces,
            own_modes[:, :rows], own_modes[:, rows:],
        ],
        0,
    )
    pieces = gathered(piece)
    inverse, near, weights = coarse_inverse(sub.astype(jnp.int32)[None], first, subs, mode_count)
    sent = search_rows(pieces, place, weights, subs)
    second = to_all(sent, SUB)

    image, own_search, own_res, turned = apply_flexibility(
        pieces, place, flex, weights, own_traces, own_modes, field, own_basis, flex_modes
    )
    second = second.reshape(subs * 2 * PAD, 128)
    low, high, direction, sums = project_direction(
        second, near, turned, image, own_search, own_res, subs, lax.axis_size(ALL)
    )
    totals = to_all(sums, ALL)
    totals = totals.sum(0)

    after = moved_along(low, -1)
    share = loads // lanes
    weights = last_weights(place, second, inverse, near, subs, mode_count, share)
    swapped = core_swap(weights)
    weights = weights + swapped
    return results(totals, direction, own_res, high, after, turned, live, along_x(weights))


def solution(mesh):
    finer = Mesh(mesh.devices.reshape(8, 4, 4, 2), ALL)
    return jax.shard_map(
        per_device,
        mesh=finer,
        in_specs=(
            P(SUB, IFC, None),
            P(SUB, None, IFC, None),
            P(SUB, None, IFC, None),
            P(SUB, None, None, IFC),
            P(SUB),
        ),
        out_specs=(P(SUB, IFC, None), P(SUB, IFC, None)),
        check_vma=False,
    )
```

```python
import jax
import jax.numpy as jnp
from jax import lax
from jax.experimental import pallas as pl
from jax.experimental.pallas import tpu as pltpu
from jax.sharding import Mesh
from jax.sharding import PartitionSpec as P


SUB = ("z", "y")
IFC = ("x", "c")
ALL = SUB + IFC
HIGH = lax.Precision.HIGHEST
NEAR = 5
PAD = 8


def dot(a, b):
    return jnp.dot(a, b, precision=HIGH, preferred_element_type=jnp.float32)


def dot_nt(a, b):
    return lax.dot_general(
        a, b, (((1,), (1,)), ((), ())), precision=HIGH, preferred_element_type=jnp.float32
    )


def inverse_kernel(subs, modes, sub_ref, sent_ref, weights_ref, inverse_ref, near_ref, cols_ref):
    lanes = 128
    for i in range(PAD):
        rows = sent_ref[pl.ds(PAD + i, subs, stride=2 * PAD), :]
        turned = jnp.concatenate([rows] * (lanes // subs), axis=0).T
        cols_ref[pl.ds(i, 3 * PAD, stride=PAD), :] = turned[: 3 * PAD]

    def column(b, j):
        start = (b * PAD + j) * PAD
        return cols_ref[start : start + PAD, :]

    sublane = lax.broadcasted_iota(jnp.int32, (PAD, lanes), 0)
    lane = lax.broadcasted_iota(jnp.int32, (PAD, lanes), 1)
    lane_mode = lane // subs
    row_sub = lax.broadcasted_iota(jnp.int32, (subs, lanes), 0)
    lane_sub = lax.broadcasted_iota(jnp.int32, (subs, lanes), 1) % subs

    def inverse(a):
        a = list(a)
        for k in range(modes):
            pivot = 1.0 / a[k][k : k + 1, :]
            is_k = sublane == k
            for j in range(modes):
                if j != k:
                    scaled = a[j][k : k + 1, :] * pivot
                    a[j] = jnp.where(is_k, scaled, a[j] - a[k] * scaled)
            a[k] = jnp.where(is_k, pivot, -a[k] * pivot)
        return a

    def product(a, b):
        out = []
        for j in range(modes):
            total = a[0] * b[j][0:1, :]
            for k in range(1, modes):
                total = total + a[k] * b[j][k : k + 1, :]
            out.append(total)
        return out

    def moved(a, shift):
        return [pltpu.roll(x, shift % lanes, 1) for x in a]

    def dense(parts):
        halves = []
        for half in range(2):
            rows_of = []
            for a, shift in parts:
                chosen = jnp.zeros((PAD, lanes), jnp.float32)
                for q in range(lanes // subs):
                    k = half * (lanes // subs) + q
                    if k < modes:
                        chosen = jnp.where(lane_mode == q, a[k], chosen)
                rows_of.append((chosen, row_sub == lane_sub + shift))
            strips = []
            for i in range(PAD):
                strip = jnp.zeros((subs, lanes), jnp.float32)
                for chosen, mask in rows_of:
                    strip = jnp.where(mask, chosen[i : i + 1, :], strip)
                strips.append(strip)
            halves.append(jnp.concatenate(strips, axis=0))
        return jnp.concatenate(halves, axis=1)

    lower = [column(0, j) for j in range(modes)]
    diag = [column(1, j) for j in range(modes)]
    upper = [column(2, j) for j in range(modes)]
    ident = [jnp.where(sublane == k, 1.0, 0.0) for k in range(modes)]
    total = None
    h = 1
    while h < subs:
        inv = inverse(diag)
        alpha = product(lower, moved(inv, h))
        gamma = product(upper, moved(inv, -h))
        upper_before, lower_before = moved(upper, h), moved(lower, h)
        upper_after, lower_after = moved(upper, -h), moved(lower, -h)
        first = product(alpha, upper_before)
        second = product(gamma, lower_after)
        diag = [d - f - g for d, f, g in zip(diag, first, second)]
        lower = [-x for x in product(alpha, lower_before)]
        upper = [-x for x in product(gamma, upper_after)]
        step = dense(
            [
                (ident, 0),
                ([-x for x in moved(alpha, -h)], h),
                ([-x for x in moved(gamma, h)], -h),
            ]
        )
        total = step if total is None else dot(step, total)
        h *= 2
    whole = dot(dense([(inverse(diag), 0)]), total)
    inverse_ref[...] = whole
    row = lax.broadcasted_iota(jnp.int32, (NEAR * PAD, PAD * subs), 0)
    col = lax.broadcasted_iota(jnp.int32, (NEAR * PAD, PAD * subs), 1)
    wanted = (row % PAD) * subs + row // PAD + (sub_ref[0] - NEAR // 2)
    inside = (row // PAD + sub_ref[0] >= NEAR // 2) & (row // PAD + sub_ref[0] < subs + NEAR // 2)
    near = dot(jnp.where((col == wanted) & inside, 1.0, 0.0), whole)
    near_ref[...] = near
    rhs = jnp.concatenate(
        [sent_ref[pl.ds(i, subs, stride=2 * PAD), :] for i in range(PAD)], axis=0
    )
    weights_ref[...] = dot(near, rhs)


def coarse_inverse(sub, sent, subs, modes):
    size = subs * PAD
    return local_call(
        lambda *refs: inverse_kernel(subs, modes, *refs),
        [(NEAR * PAD, 128), (size, size), (NEAR * PAD, size)], 1, [sent], [sub],
        [(3 * PAD * PAD, 128)],
    )


def each_piece(pieces, place_ref, copy):
    count = len(pieces) // 2
    for d in range(count):
        q = lax.rem(place_ref[0] - d + count, count)
        copy(pieces[d], 2 * q + place_ref[1])
        copy(pieces[count + d], 2 * q + 1 - place_ref[1])


def dot3(a, b):
    a_high, b_high = a.astype(jnp.bfloat16), b.astype(jnp.bfloat16)
    a_low = (a - a_high.astype(jnp.float32)).astype(jnp.bfloat16)
    b_low = (b - b_high.astype(jnp.float32)).astype(jnp.bfloat16)

    def part(x, y):
        return jnp.dot(x, y, preferred_element_type=jnp.float32)

    return part(a_high, b_high) + (part(a_high, b_low) + part(a_low, b_high))


def turned_into(ext_ref, rows_ref, count):
    filler = jnp.zeros((128 - rows_ref.shape[0], 128), jnp.float32)
    for at in range(count):
        lanes = slice(at * 128, (at + 1) * 128)
        ext_ref[lanes, 128:] = jnp.concatenate([rows_ref[:, lanes], filler], 0).T


VMEM = pl.BlockSpec(memory_space=pltpu.VMEM)
SMEM = pl.BlockSpec(memory_space=pltpu.SMEM)
ANY = pl.BlockSpec(memory_space=pl.ANY)


KERNEL_BYTES = 24 << 20


def local_call(kernel, outs, kept, arrays, scalars=(), scratch=(), far=(), free=(), large=(), sent=()):
    wait = [pltpu.SemaphoreType.DMA] if large else []

    def out_shape(k, dims):
        if k in sent:
            return jax.ShapeDtypeStruct(dims, jnp.float32)
        return (pltpu.VMEM if k < kept else pltpu.HBM)(dims, jnp.float32)

    def placed(k, a):
        if k in free:
            return a
        where = pltpu.HBM if k in large or k in far else pltpu.VMEM
        return pltpu.with_memory_space_constraint(a, where)

    return pl.pallas_call(
        kernel,
        out_shape=[out_shape(k, d) for k, d in enumerate(outs)],
        in_specs=[SMEM] * len(scalars)
        + [ANY if k in large else VMEM for k in range(len(arrays))],
        out_specs=[VMEM] * len(outs),
        scratch_shapes=[pltpu.VMEM(d, jnp.float32) for d in scratch] + wait,
        compiler_params=pltpu.CompilerParams(vmem_limit_bytes=KERNEL_BYTES),
    )(*scalars, *[placed(k, a) for k, a in enumerate(arrays)])


def stiff_kernel(rows, count, place_ref, *refs):
    pieces, refs = refs[: 2 * count], refs[2 * count :]
    rest_ref, stiff_ref, up_ref, down_ref, image_ref, basis_ref, sent_ref, ext_ref, held_ref, sem = refs
    fetch = pltpu.make_async_copy(stiff_ref, held_ref, sem)
    fetch.start()
    face = 2 * count * rows
    basis_ref[2 * PAD :, :face] = jnp.zeros((PAD, face), jnp.float32)
    basis_ref[:PAD, face:] = jnp.zeros((PAD, face), jnp.float32)

    def copy(ref, at):
        for side in range(2):
            start = pl.multiple_of(side * face + at * rows, rows)
            ext_ref[pl.ds(start, rows), :128] = ref[side * rows : (side + 1) * rows, :]
        lanes = pl.ds(pl.multiple_of(at * rows, rows), rows)
        basis_ref[: 2 * PAD, lanes] = ref[2 * rows : 2 * rows + 2 * PAD, :]
        lanes = pl.ds(pl.multiple_of(face + at * rows, rows), rows)
        basis_ref[PAD:, lanes] = ref[2 * rows + 2 * PAD :, :]

    each_piece(pieces, place_ref, copy)
    turned_into(ext_ref, basis_ref, 2 * face // 128)
    ext = ext_ref[...]
    coarse = dot(basis_ref[PAD : 2 * PAD, :], ext)
    coarse = jnp.concatenate([coarse[:, :128], coarse[:, 128:] + rest_ref[...]], 0)
    for t in range(sent_ref.shape[0]):
        sent_ref[t] = coarse
    fetch.wait()
    image = 0.25 * dot3(held_ref[...], ext)
    modes_image = image[:, 128:].T[: 3 * PAD]
    up_ref[:rows] = image[rows:, :128]
    up_ref[rows:] = modes_image[:, rows:]
    down_ref[:rows] = image[:rows, :128]
    down_ref[rows:] = modes_image[:, :rows]
    image_ref[...] = modes_image


def apply_stiffness(pieces, place, rest, stiff, subs):
    rows, face = stiff.shape[0] // 2, stiff.shape[1] // 2
    return local_call(
        lambda *refs: stiff_kernel(rows, len(pieces) // 2, *refs),
        [
            (rows + 3 * PAD, 128), (rows + 3 * PAD, 128), (3 * PAD, 2 * rows), (3 * PAD, 2 * face),
            (subs, 2 * PAD, 128),
        ],
        4, [*pieces, rest, stiff], [place], [(2 * face, 256), stiff.shape], large=[len(pieces) + 1],
        sent=[4],
    )


def search_kernel(share, place_ref, *refs):
    pieces, (weights_ref, sent_ref) = refs[:-2], refs[-2:]
    wide = NEAR * PAD
    sums = pieces[0][: 8 * PAD, :]
    for ref in pieces[1:]:
        sums = sums + ref[: 8 * PAD, :]
    weights = jnp.concatenate([weights_ref[...], jnp.zeros((128 - wide, 128), jnp.float32)], 0)
    rows = sums[: 4 * PAD] - dot(sums[4 * PAD :], weights)
    lane = lax.broadcasted_iota(jnp.int32, (PAD, 128), 1)
    mine = (place_ref[0] * 2 + place_ref[1]) * share
    tail = jnp.zeros((PAD, 128), jnp.float32)
    for b in range(3):
        block = rows[b * PAD : (b + 1) * PAD]
        block = pltpu.roll(block, lax.rem(128 - mine + b * share, 128), 1)
        tail = jnp.where(lane // share == b, block, tail)
    for b in range(3):
        low = 3 * share + b * 3 * PAD
        block = pltpu.roll(sums[(4 + b) * PAD : (5 + b) * PAD], (low - wide) % 128, 1)
        tail = jnp.where((lane >= low) & (lane < low + 3 * PAD), block, tail)
    sent = jnp.concatenate([rows[3 * PAD :], tail], 0)
    for t in range(sent_ref.shape[0]):
        sent_ref[t] = sent


def search_rows(pieces, place, weights, subs):
    return local_call(
        lambda *refs: search_kernel(128 // len(pieces), *refs),
        [(subs, 2 * PAD, 128)], 0, [*pieces, weights], [place], sent=[0],
    )[0]


def flex_kernel(rows, count, place_ref, *refs):
    pieces, refs = refs[: 2 * count], refs[2 * count :]
    flex_ref, weights_ref, own_ref, own_modes_ref, field_ref, own_basis_ref, flex_modes_ref = refs[:7]
    image_ref, search_ref, res_ref, turned_ref, ext_ref, held_ref, sem = refs[7:]
    fetch = pltpu.make_async_copy(flex_ref, held_ref, sem)
    fetch.start()
    face = 2 * count * rows
    wide = NEAR * PAD
    head = 8 * PAD
    weights = jnp.concatenate([weights_ref[...], jnp.zeros((128 - wide, 128), jnp.float32)], 0)
    filler = jnp.zeros((128 - wide, rows), jnp.float32)

    def copy(ref, at):
        for side in range(2):
            at_rows = pl.ds(pl.multiple_of(side * face + at * rows, rows), rows)
            ext_ref[at_rows, :128] = ref[head + side * rows : head + (side + 1) * rows, :]
            low = head + 2 * rows + side * wide
            ext_ref[at_rows, 128:] = jnp.concatenate([ref[low : low + wide, :], filler], 0).T

    each_piece(pieces, place_ref, copy)
    fetch.wait()
    both = dot3(held_ref[...], ext_ref[...])
    image_ref[...] = both[:, :128] - dot(both[:, 128:], weights)
    own_modes = jnp.concatenate(
        [own_modes_ref[...], jnp.zeros((128 - wide, 2 * rows), jnp.float32)], 0
    ).T
    search_ref[...] = own_ref[...] - dot(own_modes, weights)
    turned = jnp.concatenate(
        [
            flex_modes_ref[...], own_basis_ref[...],
            jnp.zeros((128 - 6 * PAD, 2 * rows), jnp.float32),
        ],
        0,
    ).T
    turned_ref[...] = turned
    gap = jnp.zeros((3 * PAD, 128), jnp.float32)
    none = jnp.zeros((128 - 6 * PAD, 128), jnp.float32)
    shifted = jnp.concatenate([gap, weights_ref[PAD : 4 * PAD, :], none], 0)
    res_ref[...] = field_ref[...] - dot(turned[rows:], shifted)


def apply_flexibility(pieces, place, flex, *arrays):
    rows, count = flex.shape[0] // 2, len(pieces)
    return local_call(
        lambda *refs: flex_kernel(rows, count // 2, *refs),
        [(2 * rows, 128), (2 * rows, 128), (rows, 128), (2 * rows, 128)], 0,
        [*pieces, flex, *arrays], [place], [(2 * count * rows, 256), flex.shape],
        free=range(count + 1, count + 1 + len(arrays)), large=[count],
    )


def chosen(a, choice):
    total = None
    for _ in range(3):
        part = a.astype(jnp.bfloat16)
        a = a - part.astype(jnp.float32)
        term = jnp.dot(part, choice, preferred_element_type=jnp.float32)
        total = term if total is None else total + term
    return total


def last_kernel(subs, modes, share, place_ref, second_ref, inverse_ref, near_ref, out_ref):
    mine = (place_ref[0] * 2 + place_ref[1]) * share
    lane = lax.broadcasted_iota(jnp.int32, (subs, 128), 1)
    row = lax.broadcasted_iota(jnp.int32, (subs, 128), 0)
    rhs = jnp.concatenate(
        [second_ref[pl.ds(i, subs, stride=2 * PAD), :] for i in range(PAD)], axis=0
    )
    weights = dot(inverse_ref[...], pltpu.roll(rhs, lax.rem(128 - mine, 128), 1))

    def earlier(x):
        return jnp.where(row == 0, 0.0, pltpu.roll(x, 1, 0))

    def later(x):
        return jnp.where(row == subs - 1, 0.0, pltpu.roll(x, subs - 1, 0))

    here = jnp.zeros((subs, 128), jnp.float32)
    for k in range(modes):
        block = weights[k * subs : (k + 1) * subs]
        here = jnp.where(lane // share == k, pltpu.roll(block, k * share, 1), here)
    near = (earlier(here), here, later(here))
    tails = jnp.concatenate(
        [second_ref[pl.ds(PAD + i, subs, stride=2 * PAD), :] for i in range(PAD)], axis=0
    )
    source = lax.broadcasted_iota(jnp.int32, (128, 9 * 128), 0)
    target = lax.broadcasted_iota(jnp.int32, (128, 9 * 128), 1)
    wanted = 3 * share + (target // 128) * PAD + (target % 128) // share
    factors = chosen(tails, (source == wanted).astype(jnp.float32).astype(jnp.bfloat16))
    products = []
    for b in range(3):
        strips = []
        for i in range(PAD):
            strip = jnp.zeros((subs, 128), jnp.float32)
            for c in range(3):
                at = (b * 3 + c) * 128
                strip = strip + factors[i * subs : (i + 1) * subs, at : at + 128] * near[c]
            strips.append(strip)
        products.append(jnp.concatenate(strips, 0))
    source = lax.broadcasted_iota(jnp.int32, (128, 128), 0)
    target = lax.broadcasted_iota(jnp.int32, (128, 128), 1)
    added = chosen(
        jnp.concatenate(products, 0),
        ((source % share == target) & (source < modes * share)).astype(jnp.float32).astype(jnp.bfloat16),
    )
    out = []
    for i in range(PAD):
        parts = []
        for b in range(3):
            tail = tails[i * subs : (i + 1) * subs]
            tail = tail if b == 0 else pltpu.roll(tail, 128 - b * share, 1)
            start = (b * PAD + i) * subs
            parts.append(tail - added[start : start + subs])
        total = parts[1] + later(parts[0]) + earlier(parts[2])
        out.append(jnp.where(lane < share, total, 0.0))
    last = dot(near_ref[PAD : 4 * PAD, :], jnp.concatenate(out, 0))
    out_ref[...] = pltpu.roll(last, mine, 1)


def last_weights(place, second, inverse, near, subs, modes, share):
    return local_call(
        lambda *refs: last_kernel(subs, modes, share, *refs),
        [(3 * PAD, 128)], 1, [second, inverse, near], [place], far=[1, 2],
    )[0]


def direction_kernel(subs, second_ref, near_ref, turned_ref, image_ref, search_ref, res_ref, low_ref, high_ref,
                     direction_ref, sums_ref):
    rows = res_ref.shape[0]
    rhs = jnp.concatenate(
        [second_ref[pl.ds(i, subs, stride=2 * PAD), :] for i in range(PAD)], axis=0
    )
    weights = dot(near_ref[PAD : 4 * PAD, :], rhs)
    none = jnp.zeros((128 - 6 * PAD, 128), jnp.float32)
    gap = jnp.zeros((3 * PAD, 128), jnp.float32)
    both = jnp.concatenate(
        [
            jnp.concatenate([weights, gap, none], 0),
            jnp.concatenate([gap, weights, none], 0),
        ],
        1,
    )
    change = dot(turned_ref[...], both)
    image = image_ref[...] - change[:, :128]
    direction = search_ref[...] - change[:, 128:]
    low_ref[...] = image[:rows]
    high_ref[...] = image[rows:]
    direction_ref[...] = direction[rows:]
    first = jnp.sum(res_ref[...] * search_ref[rows:, :], axis=0, keepdims=True)
    second = jnp.sum(direction * image, axis=0, keepdims=True)
    sums_ref[...] = jnp.broadcast_to(jnp.concatenate([first, second], 0)[None], sums_ref.shape)


def project_direction(second, near, turned, image, search, res, subs, devices):
    rows = res.shape[0]
    return local_call(
        lambda *refs: direction_kernel(subs, *refs),
        [(rows, 128), (rows, 128), (rows, 128), (devices, 2, 128)], 3,
        [second, near, turned, image, search, res], far=range(1, 6), sent=[3],
    )


def result_kernel(live_ref, totals_ref, direction_ref, res_ref, high_ref, after_ref, turned_ref, *refs):
    parts, (multipliers_ref, residual_ref) = refs[:-2], refs[-2:]
    weights = parts[0][...]
    for part in parts[1:]:
        weights = weights + part[...]
    rows = res_ref.shape[0]
    gap = jnp.zeros((3 * PAD, 128), jnp.float32)
    none = jnp.zeros((128 - 6 * PAD, 128), jnp.float32)
    change = dot(turned_ref[rows:, :], jnp.concatenate([gap, weights, none], 0))
    step = totals_ref[0:1, :] / totals_ref[1:2, :]
    image = (high_ref[...] - after_ref[...]) * live_ref[0] - change
    multipliers_ref[0] = step * direction_ref[...]
    residual_ref[0] = res_ref[...] - step * image


def results(totals, direction, res, high, after, turned, live, parts):
    return local_call(
        result_kernel, [(1, *res.shape)] * 2, 0,
        [totals, direction, res, high, after, turned, *parts], [live[None]], free=[2, 5], sent=[0, 1],
    )


def moved_along(block, distance):
    n = lax.axis_size(SUB)
    return lax.ppermute(
        block, SUB, [(i - distance, i) for i in range(n) if 0 <= i - distance < n]
    )


def core_swap(block):
    return lax.ppermute(block, "c", [(0, 1), (1, 0)])


def along_x(piece):
    n = lax.axis_size("x")
    return [piece] + [
        lax.ppermute(piece, "x", [(i, (i + d) % n) for i in range(n)]) for d in range(1, n)
    ]


def to_all(values, axis):
    return lax.all_to_all(values, axis, 0, 0, tiled=True)


def gathered(piece):
    pieces = along_x(piece)
    return pieces + [core_swap(part) for part in pieces]


def per_device(gap, flexibility, stiffness, modes, mode_counts):
    subs = lax.axis_size(SUB)
    sub = lax.axis_index(SUB)
    place = jnp.stack([lax.axis_index("x"), lax.axis_index("c")]).astype(jnp.int32)
    rows, loads = gap.shape[1], gap.shape[2]
    lanes = lax.axis_size(IFC)
    face = rows * lanes
    mode_count = modes.shape[1]
    live = (sub < subs - 1).astype(jnp.float32)
    inner = (sub > 0).astype(jnp.float32)
    flex = flexibility.reshape(2 * rows, 2 * face)
    stiff = stiffness.reshape(2 * rows, 2 * face)

    active = (jnp.arange(PAD) < jnp.minimum(mode_counts[0], mode_count)).astype(jnp.float32)
    padded = jnp.pad(modes[0], ((0, PAD - mode_count), (0, 0), (0, 0))) * active[:, None, None]
    left, right = padded[:, 0], padded[:, 1] * live
    field = gap[0] * live

    from_before = moved_along(jnp.concatenate([field, right], 0), 1)
    left_after = moved_along(left, -1)
    field_before, right_before = from_before[:rows], from_before[rows:]
    left_in = left * inner
    piece = jnp.concatenate([-field_before, field, -right_before, left_in, right, -left_after], 0)
    none = jnp.zeros_like(left)
    own_basis = jnp.concatenate(
        [
            jnp.concatenate([-right_before, left_in, none], 0),
            jnp.concatenate([none, right, -left_after], 0),
        ],
        1,
    )
    rest = jnp.pad(
        jnp.eye(PAD, dtype=jnp.float32) * (1.0 - active)[:, None], ((0, 0), (PAD, 128 - 2 * PAD))
    )
    up, down, modes_image, basis, sent = apply_stiffness(gathered(piece), place, rest, stiff, subs)
    first = to_all(sent, SUB).reshape(subs * 2 * PAD, 128)
    before = moved_along(up, 1)
    after = moved_along(down, -1)
    top = (down[:rows] - before[:rows]) * inner
    bottom = (up[:rows] - after[:rows]) * live
    own_traces = jnp.concatenate([top, bottom], 0)
    gone = jnp.zeros((PAD, rows), jnp.float32)
    modes_top = jnp.concatenate([gone, modes_image[:, :rows], gone], 0)
    modes_top = modes_top - jnp.concatenate([before[rows:], gone, gone], 0)
    modes_bottom = jnp.concatenate([gone, modes_image[:, rows:], gone], 0)
    modes_bottom = modes_bottom - jnp.concatenate([gone, gone, after[rows:]], 0)
    own_modes = jnp.concatenate([modes_top * inner, modes_bottom * live], 1)

    flex_modes = dot_nt(basis, flex)
    tests = jnp.concatenate([flex_modes, own_basis[PAD : 2 * PAD]], 0)
    small = dot_nt(tests, jnp.concatenate([own_modes, own_basis], 0))
    piece = jnp.concatenate(
        [
            dot(tests, own_traces), jnp.pad(small, ((0, 0), (0, 128 - small.shape[1]))), own_traces,
            own_modes[:, :rows], own_modes[:, rows:],
        ],
        0,
    )
    pieces = gathered(piece)
    weights, inverse, near = coarse_inverse(sub.astype(jnp.int32)[None], first, subs, mode_count)
    sent = search_rows(pieces, place, weights, subs)
    second = to_all(sent, SUB)

    image, own_search, own_res, turned = apply_flexibility(
        pieces, place, flex, weights, own_traces, own_modes, field, own_basis, flex_modes
    )
    second = second.reshape(subs * 2 * PAD, 128)
    low, high, direction, sums = project_direction(
        second, near, turned, image, own_search, own_res, subs, lax.axis_size(ALL)
    )
    totals = to_all(sums, ALL)
    totals = totals.sum(0)

    after = moved_along(low, -1)
    share = loads // lanes
    weights = last_weights(place, second, inverse, near, subs, mode_count, share)
    swapped = core_swap(weights)
    weights = weights + swapped
    return results(totals, direction, own_res, high, after, turned, live, along_x(weights))


def solution(mesh):
    finer = Mesh(mesh.devices.reshape(8, 4, 4, 2), ALL)
    return jax.shard_map(
        per_device,
        mesh=finer,
        in_specs=(
            P(SUB, IFC, None),
            P(SUB, None, IFC, None),
            P(SUB, None, IFC, None),
            P(SUB, None, None, IFC),
            P(SUB),
        ),
        out_specs=(P(SUB, IFC, None), P(SUB, IFC, None)),
        check_vma=False,
    )
```
